256 devices in a mesh: shot: 4 (over x), band: 32 (over y_lo, z, core), net: 2 (over y_hi).
Axes of the slice: x: 4, y: 4 (y_hi: 2, y_lo: 2; y = y_hi * 2 + y_lo), z: 8, core: 2. Of those that a mesh axis runs over, the one named last changes fastest.
Arguments:
- velocity: float32 [1024, 1024], P('band'), may hold values from 1.5 to 4
- wave_now: float32 [16, 1024, 1024], P(('shot', 'net'), 'band'), may hold values from -6 to 6
- wave_before: float32 [16, 1024, 1024], P(('shot', 'net'), 'band'), may hold values from -6 to 6
- adjoint_last: float32 [16, 1024, 1024], P(('shot', 'net'), 'band'), may hold values from -6 to 6
- adjoint_after: float32 [16, 1024, 1024], P(('shot', 'net'), 'band'), may hold values from -6 to 6
- wavelet: float32 [16, 16], P(('shot', 'net')), may hold values from -72 to 72
- source_col: int32 [16], P(('shot', 'net')), may hold values from 0 to 1023
- rec_first: int32 [16], P(('shot', 'net')), may hold values from 0 to 1022
- rec_last: int32 [16], P(('shot', 'net')), may hold values from 1 to 1023
- rec_count: int32 [16], P(('shot', 'net')), may hold values from 2 to 128, as said below
- observed: float32 [16, 16, 128], P(('shot', 'net')), may hold values from -72 to 72
- conv_in: float32 [32, 18], replicated, may hold values from -1.5 to 1.5
- conv_mid: float32 [32, 288], replicated, may hold values from -0.375 to 0.375
- conv_out: float32 [1, 288], replicated, may hold values from -0.375 to 0.375
- cotangent: float32 [1024, 1024], P('band', ('shot', 'net')), may hold values from -0.0234375 to 0.0234375
Outputs:
- new_velocity: float32 [1024, 1024], P('band', ('shot', 'net'))
- grad_in: float32 [32, 18], replicated
- grad_mid: float32 [32, 288], replicated
- grad_out: float32 [1, 288], replicated
The draws below stay inside these ranges and needn't reach their ends.
Inputs may be any that keep to these rules, and one draw needn't show every extreme that they name: rec_last - rec_first >= rec_count - 1 for every shot; some shot has 128 receivers.
All inputs are finite; a program needn't handle non-finite values.
Results may differ from the reference program's by a relative error of at most 0.0003.
Values sent between devices are 32-bit elements; how exact they have to be, the bound alone decides.
No kernel may reach another device: no remote copies, remote signals or barrier semaphores. Data moves between devices by JAX's collectives and lax.ppermute only.
A program may use at most 128 MiB of HBM per device.

```python
import math
import jax
import jax.numpy as jnp
from jax import lax

NT = 16
CH = 32
MAXREC = 128
NX = 1024
NZ = 1024
SHOTS = 16


def receiver_draw(key):
    keys = jax.random.split(jax.random.fold_in(key, 7), 4)
    shot_ids = jnp.arange(SHOTS)
    chosen = jax.random.randint(keys[3], (), 0, SHOTS)
    fullest = shot_ids == chosen
    rightmost = shot_ids == (chosen + 1) % SHOTS
    leftmost = shot_ids == (chosen + 2) % SHOTS
    narrow = rightmost | leftmost
    counted = jax.random.randint(keys[0], (SHOTS,), 2, MAXREC + 1)
    counted = jnp.where(fullest, MAXREC, jnp.where(narrow, 2, counted))
    extra = jax.random.randint(keys[1], (SHOTS,), 0, NZ - counted + 1)
    span = jnp.where(narrow, 1, counted - 1 + extra)
    starts = jax.random.randint(keys[2], (SHOTS,), 0, NZ - span)
    starts = jnp.where(rightmost, NZ - 2, jnp.where(leftmost, 0, starts))
    return (starts.astype(jnp.int32), (starts + span).astype(jnp.int32), counted.astype(jnp.int32))


def draw_rec_first(key, part):
    return receiver_draw(key)[0]


def draw_rec_last(key, part):
    return receiver_draw(key)[1]


def draw_rec_count(key, part):
    return receiver_draw(key)[2]


def with_ends(values, rng, low, high):
    spot = [jax.random.randint(jax.random.fold_in(rng, axis), (), 0, length) for axis, length in enumerate(values.shape)]
    main_axis = values.shape.index(max(values.shape))
    next_to = spot[:main_axis] + [(spot[main_axis] + 1) % values.shape[main_axis]] + spot[main_axis + 1:]
    return values.at[tuple(spot)].set(low).at[tuple(next_to)].set(high)


def block_levels(own_key, extent, cuts, low, largest):
    def one(position, parts):
        draws = jax.random.uniform(jax.random.fold_in(jax.random.fold_in(own_key, 6), position), (parts,), jnp.float32, low / len(cuts), largest / len(cuts))
        return jnp.repeat(jnp.exp(draws), extent[position] // parts).reshape((-1,) + (1,) * (len(extent) - position - 1))

    factor_of = one(*cuts[0])
    for cut in cuts[1:]:
        factor_of = factor_of * one(*cut)
    return factor_of


def noise(key, shape, spread, bound, pieces=(), held_as=jnp.bfloat16):
    gain = block_levels(key, shape, pieces, -0.22, 0.18) if pieces else 1.0
    array = jax.random.normal(key, shape, jnp.float32) * spread * gain
    return jnp.minimum(jnp.maximum(array, -bound), bound).astype(held_as)


def setup_inputs(seed: int = 0) -> dict:
    key_list = jax.random.split(jax.random.key(seed), 16)
    velocity = jnp.clip(jnp.exp(math.log(4.0) - 0.98082925 * jax.random.uniform(key_list[0], (NX, NZ), jnp.float32) ** block_levels(key_list[0], (NX, NZ), ((0, 32),), -0.2, 0.2)), 1.5, 4.0)
    wave_now = noise(key_list[1], (SHOTS, NX, NZ), 1.0, 6.0, ((0, 8), (1, 32)), jnp.float32)
    wave_before = noise(key_list[2], (SHOTS, NX, NZ), 1.0, 6.0, ((0, 8), (1, 32)), jnp.float32)
    adjoint_last = noise(key_list[3], (SHOTS, NX, NZ), 1.0, 6.0, ((0, 8), (1, 32)), jnp.float32)
    adjoint_after = noise(key_list[4], (SHOTS, NX, NZ), 1.0, 6.0, ((0, 8), (1, 32)), jnp.float32)
    wavelet = noise(key_list[5], (SHOTS, NT), 12.0, 72.0, ((0, 8),), jnp.float32)
    source_col = with_ends(jax.random.randint(key_list[6], (SHOTS,), 0, NZ), jax.random.fold_in(key_list[6], 1), 0, NZ - 1).astype(jnp.int32)
    rec_first = draw_rec_first(jax.random.fold_in(key_list[15], 71), 0)
    rec_last = draw_rec_last(jax.random.fold_in(key_list[15], 71), 0)
    rec_count = draw_rec_count(jax.random.fold_in(key_list[15], 71), 0)
    observed = noise(key_list[10], (SHOTS, NT, MAXREC), 12.0, 72.0, ((0, 8),), jnp.float32)
    conv_in = noise(key_list[11], (CH, 18), 18 ** -0.5, 1.5, (), jnp.float32)
    conv_mid = noise(key_list[12], (CH, 9 * CH), (9 * CH) ** -0.5, 0.375, (), jnp.float32)
    conv_out = noise(key_list[13], (1, 9 * CH), (9 * CH) ** -0.5, 0.375, (), jnp.float32)
    cotangent = noise(key_list[14], (NX, NZ), (4.0 / (NX * NZ) ** 0.5), 0.0234375, ((0, 32), (1, 8)), jnp.float32)
    return {"velocity": velocity, "wave_now": wave_now, "wave_before": wave_before, "adjoint_last": adjoint_last, "adjoint_after": adjoint_after, "wavelet": wavelet, "source_col": source_col, "rec_first": rec_first, "rec_last": rec_last, "rec_count": rec_count, "observed": observed, "conv_in": conv_in, "conv_mid": conv_mid, "conv_out": conv_out, "cotangent": cotangent}


coefficients = (-205.0 / 72.0, 8.0 / 5.0, -1.0 / 5.0, 8.0 / 315.0, -1.0 / 560.0)
speed_factor = 0.11
source_depth = 2
receiver_depth = 3
highest = lax.Precision.HIGHEST

def laplace(extended):
    middle = extended[..., 4:-4, :]
    height = middle.shape[-2]
    breadth = middle.shape[-1]
    padding = [(0, 0)] * (middle.ndim - 1) + [(4, 4)]
    padded = jnp.pad(middle, padding)
    running = 2.0 * coefficients[0] * middle
    for reach in range(1, 5):
        vertical = extended[..., 4 - reach:4 - reach + height, :] + extended[..., 4 + reach:4 + reach + height, :]
        lateral = padded[..., 4 - reach:4 - reach + breadth] + padded[..., 4 + reach:4 + reach + breadth]
        running = running + coefficients[reach] * (vertical + lateral)
    return running

def receiver_table(rec_first, rec_last, rec_count, breadth, slots):
    columns = jnp.arange(breadth, dtype=jnp.int32)
    slot_ids = jnp.arange(slots, dtype=jnp.int32)
    placed = rec_first[:, None] + slot_ids[None, :] * (rec_last - rec_first)[:, None] // (rec_count - 1)[:, None]
    active = slot_ids[None, :] < rec_count[:, None]
    return ((columns[None, :, None] == placed[:, None, :]) & active[:, None, :]).astype(jnp.float32)

def convolve(field, weights):
    outputs = weights.shape[0]
    channels = field.shape[0]
    kernel = weights.reshape(outputs, 3, 3, channels).transpose(0, 3, 1, 2)
    return lax.conv_general_dilated(field[None], kernel, (1, 1), ((1, 1), (1, 1)), precision=highest)[0]

def network(first_weights, middle_weights, last_weights, velocity, scaled):
    layer_zero = jnp.stack([velocity, scaled])
    hidden_one = jax.nn.silu(convolve(layer_zero, first_weights))
    hidden_two = jax.nn.silu(convolve(hidden_one, middle_weights))
    return velocity + convolve(hidden_two, last_weights)[0]

def reference(velocity, wave_now, wave_before, adjoint_last, adjoint_after, wavelet, source_col, rec_first, rec_last, rec_count, observed, conv_in, conv_mid, conv_out, cotangent):
    speed_sq = (velocity * speed_factor) ** 2
    rows_all = jnp.arange(NX, dtype=jnp.int32)
    columns = jnp.arange(NZ, dtype=jnp.int32)
    source_rows = (rows_all == source_depth).astype(jnp.float32)[:, None]
    receiver_rows = (rows_all == receiver_depth).astype(jnp.float32)[:, None]
    tables = receiver_table(rec_first, rec_last, rec_count, NZ, MAXREC)
    active = (jnp.arange(MAXREC, dtype=jnp.int32)[None, :] < rec_count[:, None]).astype(jnp.float32)

    def advance(current, earlier, term):
        extended = jnp.pad(current, ((4, 4), (0, 0)))
        return 2.0 * current - earlier + speed_sq * laplace(extended) + term

    def one_shot(running, shot):
        start, prior, adjoint_start, adjoint_prior, pulses, place, table, recorded, live = shot
        source_field = source_rows * (columns == place).astype(jnp.float32)[None, :]

        def forward(carry, amount):
            fresh = advance(carry[0], carry[1], amount * source_field)
            return ((fresh, carry[0]), fresh)
        ignored, stored = lax.scan(forward, (start, prior), pulses)
        samples = jnp.dot(stored[:, receiver_depth, :], table, precision=highest)
        misfit = (samples - recorded) * live[None, :]

        def backward(carry, inputs):
            field, residual = inputs
            injected = receiver_rows * jnp.dot(table, residual, precision=highest)[None, :]
            fresh = advance(carry[0], carry[1], injected)
            return ((fresh, carry[0], carry[2] + field * fresh), None)
        final, unused = lax.scan(backward, (adjoint_start, adjoint_prior, running), (stored, misfit), reverse=True)
        return (final[2], None)
    image, ignored = lax.scan(one_shot, jnp.zeros((NX, NZ), jnp.float32), (wave_now, wave_before, adjoint_last, adjoint_after, wavelet, source_col, tables, observed, active))
    scaled = image / float(NT * SHOTS) ** 0.5

    def apply(first_weights, middle_weights, last_weights):
        return network(first_weights, middle_weights, last_weights, velocity, scaled)
    new_velocity, pullback = jax.vjp(apply, conv_in, conv_mid, conv_out)
    grads = pullback(cotangent)
    return (new_velocity, grads[0], grads[1], grads[2])
```

```python
import numpy as np

import jax
import jax.numpy as jnp
from jax import lax
from jax.experimental import pallas as pl
from jax.experimental.pallas import tpu as pltpu
from jax.sharding import Mesh
from jax.sharding import PartitionSpec as P

BAND = ("band_0", "band_1", "band_2")
CHIPS = ("band_0", "band_1")
CORE = "band_2"
CELL = ("shot", "net")
SUMMED = ("shot", "band_2", "net")

coefficients = (-205.0 / 72.0, 8.0 / 5.0, -1.0 / 5.0, 8.0 / 315.0, -1.0 / 560.0)
speed_factor = 0.11
source_depth = 2
receiver_depth = 3
highest = lax.Precision.HIGHEST

STEPS = 16
CHIP = 64
WIDE = 3 * CHIP
LINE = 136
FLAT = 42 * 128
PART = 768
SIDE = 256
CH = 32
vmem_limit = 56 * 1024 * 1024
TAPS = [(down - 1) * LINE + (across - 1) for down in range(3) for across in range(3)]


def stencil_constants():
    lane = lax.broadcasted_iota(jnp.int32, (8, 128), 1)
    column = lax.broadcasted_iota(jnp.int32, (8, 128), 0) * 128 + lane
    c0, c1, c2, c3, c4 = coefficients

    def where(mask, value):
        return jnp.where(mask, jnp.float32(value), jnp.float32(0.0))

    return dict(
        low1=lane < 1,
        low3=lane < 3,
        high1=lane >= 127,
        high3=lane >= 125,
        c1u=where(column != 0, c1),
        c1v=where(column != 1023, c1),
        c2p=where((column != 1021) & (column != 1022), c2),
        c3p=where(column <= 1020, c3),
        c4p=where((column <= 1020) & (column != 0), c4),
        c2m=where((column != 1) & (column != 2), c2),
        c3m=where(column >= 3, c3),
        c4m=where((column >= 3) & (column != 1023), c4),
    )


def from_left(x, count, mask):
    turned = pltpu.roll(x, count, 1)
    return jnp.where(mask, pltpu.roll(turned, 1, 0), turned)


def from_right(x, count, mask):
    turned = pltpu.roll(x, 128 - count, 1)
    return jnp.where(mask, pltpu.roll(turned, 7, 0), turned)


def next_row(k, rows, at, prior, speed):
    x = rows[at]
    left = from_left(x, 1, k["low1"])
    right = from_right(x, 1, k["high1"])
    ahead = k["c2p"] * right + k["c3p"] * x + k["c4p"] * left
    behind = k["c2m"] * left + k["c3m"] * x + k["c4m"] * right
    total = k["c1u"] * left + k["c1v"] * right
    total = total + from_left(ahead, 3, k["low3"])
    total = total + from_right(behind, 3, k["high3"])
    vertical = (2.0 * coefficients[0]) * x
    for reach in range(1, 5):
        vertical = vertical + coefficients[reach] * (rows[at - reach] + rows[at + reach])
    return (x + x) - prior + speed * (total + vertical)


def advance(k, fields, speeds, now, step, after_core):
    other = 1 - now

    def block(first, count, store_more=None):
        rows = [fields[now, first - 4 + i] for i in range(count + 8)]
        for i in range(count):
            fresh = next_row(k, rows, i + 4, fields[other, first + i], speeds[first + i])
            fields[other, first + i] = fresh
            if store_more is not None:
                store_more(first - CHIP + i, fresh)

    reach = 4 * step

    def sides(i, carry):
        block(reach + 4 * i, 4)
        block(2 * CHIP + 4 * i, 4)
        return carry

    if step < STEPS:
        lax.fori_loop(0, STEPS - step, sides, 0)

    def core(i, carry):
        block(CHIP + 8 * i, 8, after_core)
        return carry

    lax.fori_loop(0, CHIP // 8, core, 0)


def fill(fields, speeds, low, mid, high, velocity_low, velocity_mid, velocity_high):
    for place, source, speed in (
        (0, low, velocity_low),
        (CHIP, mid, velocity_mid),
        (2 * CHIP, high, velocity_high),
    ):

        def copy(i, carry, place=place, source=source, speed=speed):
            for part in range(2):
                fields[part, pl.ds(place + 8 * i, 8)] = source[pl.ds(CHIP * part + 8 * i, 8)]
            speeds[pl.ds(place + 8 * i, 8)] = speed(8 * i)
            return carry

        lax.fori_loop(0, CHIP // 8, copy, 0)


def squared(values):
    scaled = values * speed_factor
    return scaled * scaled


def forward_kernel(pulses, source, low, mid, velocity, high, stored, speeds, fields):
    def halo_speed(ref):
        return lambda first: squared(ref[pl.ds(2 * CHIP + first, 8)])

    fill(
        fields,
        speeds,
        low,
        mid,
        high,
        halo_speed(low),
        lambda first: squared(velocity[pl.ds(first, 8)]),
        halo_speed(high),
    )
    k = stencil_constants()
    for n in range(STEPS):
        now = n % 2

        def keep(row, fresh, n=n):
            stored[n, row] = fresh

        advance(k, fields, speeds, now, n + 1, keep)
        row = CHIP + source_depth
        fresh = fields[1 - now, row] + pulses[n] * source[...]
        fields[1 - now, row] = fresh
        stored[n, source_depth] = fresh


def adjoint_kernel(counts, recorded, low, mid, high, speeds_in, stored, extra, out, fields, image, turned):
    for place, source in ((0, low), (CHIP, mid), (2 * CHIP, high)):

        def copy(i, carry, place=place, source=source):
            for part in range(2):
                fields[part, pl.ds(place + 8 * i, 8)] = source[pl.ds(CHIP * part + 8 * i, 8)]
            return carry

        lax.fori_loop(0, CHIP // 8, copy, 0)
    k = stencil_constants()

    def image_at(row):
        return (pl.ds(pl.multiple_of(row * 8, 8), 8), slice(None))

    for m in range(STEPS):
        now = m % 2
        n = STEPS - 1 - m

        def add(row, fresh, n=n, m=m):
            product = stored[n, row] * fresh
            if m:
                product = image[image_at(row)] + product
            image[image_at(row)] = product

        advance(k, fields, speeds_in, now, m + 1, add)
        row = CHIP + receiver_depth
        sample = stored[n, receiver_depth]
        push = counts[...] * sample - recorded[n]
        fields[1 - now, row] = fields[1 - now, row] + push
        place = image_at(receiver_depth)
        image[place] = image[place] + sample * push
    blank = jnp.zeros((64, 128), jnp.float32)
    for j in range(8):
        block = jnp.concatenate(
            [image[pl.ds(64 * b + j, 8, stride=8), :] for b in range(8)], axis=0
        )
        for core in range(2):
            d = ((j // 2) * 2 + core) * 2 + j % 2
            out[d, 0:40, :] = block[24 * core : 24 * core + 40]
        turned[j] = jnp.transpose(jnp.concatenate([block, blank], axis=0))
    sub = lax.broadcasted_iota(jnp.int32, (8, 128), 0)
    for j in range(8):
        edges = jnp.zeros((8, 128), jnp.float32)
        if j > 0:
            edges = jnp.where(sub < 3, pltpu.roll(turned[j - 1, 120:128, :], 3, 0), edges)
        if j < 7:
            edges = jnp.where(
                (sub >= 3) & (sub < 6), pltpu.roll(turned[j + 1, 0:8, :], 3, 0), edges
            )
        for core in range(2):
            d = ((j // 2) * 2 + core) * 2 + j % 2
            out[d, 40:48, :] = edges + extra[d]


def split(x):
    high = x.astype(jnp.bfloat16)
    low = (x - high.astype(jnp.float32)).astype(jnp.bfloat16)
    return high, low


def window(ref, rows, first, count, shift):
    start = SIDE + first + shift
    base = start // 128 * 128
    offset = start - base
    if offset == 0:
        return ref[rows, base : base + count]
    wide = ref[rows, base : base + count + 128]
    return pltpu.roll(wide, count + 128 - offset, 1)[:, :count]


def mul(left, right):
    return jnp.dot(left, right, preferred_element_type=jnp.float32)


def mul_t(left, right):
    return lax.dot_general(
        left, right, (((1,), (1,)), ((), ())), preferred_element_type=jnp.float32
    )


def network_kernel(
    core, summed, arrived, velocity_wide, cotangent_rows, inside, own, first_w, middle_w, back_w, last_w,
    new_velocity, grads,
    base, taps, packed, slope_one_d, before, products, last_products, pairs, hidden_one, slope_own, packed_two, packed_slope, own_terms, updates,
):
    lane = lax.broadcasted_iota(jnp.int32, (8, 128), 1)
    sub = lax.broadcasted_iota(jnp.int32, (8, 128), 0)
    lower = core[0] == 0
    edges = summed[40:48, :]
    other_edges = arrived[8:16, :]
    edge_rows = jnp.where(
        lower,
        jnp.where(lane < 3, pltpu.roll(other_edges, 67, 1), pltpu.roll(edges, 3, 1)),
        jnp.where(
            (lane >= 35) & (lane < 38), pltpu.roll(other_edges, 35, 1), pltpu.roll(edges, 99, 1)
        ),
    )
    turned = jnp.transpose(
        jnp.concatenate(
            [edge_rows, pltpu.roll(edges, 65, 1), jnp.zeros((112, 128), jnp.float32)], axis=0
        )
    )[0:40]
    main = summed[0:40, :]
    tile = pltpu.roll(arrived[0:8, :], 3, 0)
    down = pltpu.roll(main, 3, 0)
    up = pltpu.roll(main, 35, 0)
    low_case = jnp.concatenate([jnp.where(sub < 3, tile, down[0:8]), down[8:40]], axis=0)
    high_case = jnp.concatenate(
        [up[0:32], jnp.where((sub >= 3) & (sub < 6), tile, up[32:40])], axis=0
    )
    image = jnp.where(lower, low_case, high_case)
    lanes = lax.broadcasted_iota(jnp.int32, (40, 128), 1)
    scale = 1.0 / float(STEPS * 16) ** 0.5
    shifted = pltpu.roll(image, 3, 1)
    image_a = jnp.where(lanes < 3, turned, shifted) * scale
    image_b = jnp.where(lanes < 3, shifted, jnp.where(lanes < 6, turned, 0.0)) * scale
    shifted = pltpu.roll(cotangent_rows[...], 3, 1)
    sides = pltpu.roll(turned, 121, 1)
    cot_a = jnp.where(lanes < 1, 0.0, jnp.where(lanes < 3, sides, shifted))
    cot_b = jnp.where(lanes < 3, shifted, jnp.where(lanes < 5, sides, 0.0))
    velocity_all = velocity_wide[...]

    base[...] = jnp.zeros(base.shape, jnp.float32)
    wide_rows = [
        velocity_all,
        jnp.concatenate([image_a, image_b], axis=1),
        jnp.concatenate([cot_a, cot_b], axis=1),
    ]
    for channel, wide in enumerate(wide_rows):
        pieces = {}
        for r in range(38):
            start = LINE * r
            v, offset = start // 128, start % 128
            row = wide[r : r + 1, :]
            if offset:
                row = pltpu.roll(row, offset, 1)
            pieces.setdefault(v, []).append(row[:, 0:128])
            pieces.setdefault(v + 1, []).append(row[:, 128:256])
        for v, found in pieces.items():
            total = found[0]
            for piece in found[1:]:
                total = total + piece
            base[channel : channel + 1, SIDE + 128 * v : SIDE + 128 * v + 128] = total

    parts = [(p * PART, slice(p * PART, (p + 1) * PART)) for p in range(FLAT // PART)]
    all_rows = slice(0, 8)
    padding = jnp.zeros((8, PART), jnp.float32)
    for first, cut in parts:
        gathered = [window(base, all_rows, first, PART, shift) for shift in TAPS]
        high, low = split(jnp.concatenate(gathered + [padding], axis=0))
        taps[0:80, cut] = high
        taps[80:160, cut] = low
        result = mul(first_w[...], taps[:, cut])
        result = result[0:64] + result[64:128]
        value = result[0:CH]
        pulled = jax.nn.sigmoid(value)
        slope_one_d[:, cut] = pulled * (1.0 + value * (1.0 - pulled))
        mask = inside[:, cut] > 0.0
        mask = jnp.concatenate([mask] * 4, axis=0)
        hidden = jnp.where(mask, value * pulled, 0.0)
        hidden_one[:, SIDE + first : SIDE + first + PART] = hidden
        before[:, cut] = result[CH : 2 * CH]
        high, low = split(hidden)
        packed[0:32, cut] = high
        packed[32:64, cut] = low
        packed[64:96, cut] = high
    edge = jnp.zeros((CH, SIDE), jnp.float32)
    hidden_one[:, 0:SIDE] = edge
    hidden_one[:, SIDE + FLAT :] = edge
    zero_edge = jnp.zeros((9 * CH, SIDE), jnp.float32)
    products[:, 0:SIDE] = zero_edge
    products[:, SIDE + FLAT :] = zero_edge
    last_products[:, 0:SIDE] = jnp.zeros((16, SIDE), jnp.float32)
    last_products[:, SIDE + FLAT :] = jnp.zeros((16, SIDE), jnp.float32)

    for first, cut in parts:
        products[:, SIDE + first : SIDE + first + PART] = mul(middle_w[...], packed[:, cut])
    for first, cut in parts:
        mask = inside[:, cut] > 0.0
        here = own[:, cut] > 0.0
        for g in range(4):
            total = None
            for tap, shift in enumerate(TAPS):
                piece = window(
                    products, slice(tap * CH + 8 * g, tap * CH + 8 * g + 8), first, PART, shift
                )
                total = piece if total is None else total + piece
            pulled = jax.nn.sigmoid(total)
            rows = slice(8 * g, 8 * g + 8)
            hidden = jnp.where(mask, total * pulled, 0.0)
            slope = jnp.where(
                mask, before[rows, cut] * (pulled * (1.0 + total * (1.0 - pulled))), 0.0
            )
            pairs[rows, cut] = hidden
            slope_own[rows, cut] = slope
        hidden = pairs[:, cut]
        slope = slope_own[:, cut]
        high, low = split(hidden)
        packed_two[0:32, cut] = high
        packed_two[32:64, cut] = low
        packed_two[64:96, cut] = high
        here = jnp.concatenate([here] * 4, axis=0)
        high, low = split(jnp.where(here, hidden, 0.0))
        own_terms[32:64, cut] = high
        own_terms[96:128, cut] = low
        high, low = split(slope)
        packed_slope[0:32, cut] = high
        packed_slope[32:64, cut] = low
        packed_slope[64:96, cut] = high
        last_products[:, SIDE + first : SIDE + first + PART] = mul(last_w[...], packed_two[:, cut])

    wide_sub = lax.broadcasted_iota(jnp.int32, (8, PART), 0)
    for first, cut in parts:
        total = jnp.zeros((8, PART), jnp.float32)
        for tap, shift in enumerate(TAPS):
            rows = slice(0, 8) if tap < 8 else slice(8, 16)
            piece = window(last_products, rows, first, PART, shift)
            total = total + jnp.where(wide_sub == tap % 8, piece, 0.0)
        updates[0:1, cut] = jnp.sum(total, axis=0, keepdims=True)
    velocity_here = pltpu.roll(velocity_all, 253, 1)[:, 0:128]
    for r in range(32):
        start = LINE * (r + 3) + 3
        v, offset = start // 128, start % 128
        row = updates[0:1, 128 * v : 128 * v + 256]
        if offset:
            row = pltpu.roll(row, 256 - offset, 1)
        new_velocity[r : r + 1, :] = velocity_here[r + 3 : r + 4] + row[:, 0:128]

    for first, cut in parts:
        products[:, SIDE + first : SIDE + first + PART] = mul(back_w[...], packed_slope[:, cut])
    for first, cut in parts:
        here = own[:, cut] > 0.0
        for g in range(4):
            total = None
            for tap, shift in enumerate(TAPS):
                piece = window(
                    products, slice(tap * CH + 8 * g, tap * CH + 8 * g + 8), first, PART, -shift
                )
                total = piece if total is None else total + piece
            rows = slice(8 * g, 8 * g + 8)
            pairs[rows, cut] = jnp.where(here, total * slope_one_d[rows, cut], 0.0)
        high, low = split(pairs[:, cut])
        own_terms[0:32, cut] = high
        own_terms[64:96, cut] = low

    middle_sum = jnp.zeros((CH, 9 * CH), jnp.float32)
    outer_sum = jnp.zeros((64, 80), jnp.float32)
    for first, cut in parts:
        here = jnp.concatenate([own[:, cut] > 0.0] * 4, axis=0)
        shifted = jnp.concatenate(
            [window(hidden_one, slice(0, CH), first, PART, shift) for shift in TAPS], axis=0
        )
        high, low = split(shifted)
        slope_high, slope_low = split(jnp.where(here, slope_own[:, cut], 0.0))
        both = mul_t(jnp.concatenate([slope_high, slope_low], axis=0), high)
        middle_sum = middle_sum + (both[0:CH] + both[CH:] + mul_t(slope_high, low))
        terms = own_terms[:, cut]
        both = mul_t(terms, taps[0:80, cut])
        outer_sum = outer_sum + (both[0:64] + both[64:128] + mul_t(terms[0:64], taps[80:160, cut]))
    grads[:, 0:288] = middle_sum
    column = lax.broadcasted_iota(jnp.int32, (CH, 80), 1)
    mixed = jnp.where(column % 8 < 2, outer_sum[0:CH], outer_sum[CH:64])
    grads[:, 384:464] = mixed


def vmem():
    return pl.BlockSpec(memory_space=pltpu.VMEM)


def smem():
    return pl.BlockSpec(memory_space=pltpu.SMEM)


def f32(*shape):
    return jax.ShapeDtypeStruct(shape, jnp.float32)


def scratch(*shape, dtype=jnp.float32):
    return pltpu.VMEM(shape, dtype)


def call(kernel, in_specs, out_shape, scratch_shapes, *operands):
    many = isinstance(out_shape, tuple)
    return pl.pallas_call(
        kernel,
        in_specs=in_specs,
        out_specs=tuple(vmem() for _ in out_shape) if many else vmem(),
        out_shape=out_shape,
        scratch_shapes=scratch_shapes,
        compiler_params=pltpu.CompilerParams(vmem_limit_bytes=vmem_limit),
    )(*operands)


def stacked_weights(weights):
    high = weights.astype(jnp.bfloat16)
    low = (weights - lax.reduce_precision(weights, 8, 7)).astype(jnp.bfloat16)
    return high, low


def three_terms(weights):
    high, low = stacked_weights(weights)
    return jnp.concatenate([high, high, low], axis=1)


def over_pairs(x, axis, groups):
    return x + lax.ppermute(x, axis, [(a, b) for a, b in groups] + [(b, a) for a, b in groups])


def over_fours(x, axis, groups):
    near, far, cross = (
        lax.ppermute(x, axis, [(group[i], group[i ^ turn]) for group in groups for i in range(4)])
        for turn in (1, 2, 3)
    )
    return (x + near) + (far + cross)


def on_device(
    velocity,
    wave_now,
    wave_before,
    adjoint_last,
    adjoint_after,
    wavelet,
    source_col,
    rec_first,
    rec_last,
    rec_count,
    observed,
    conv_in,
    conv_mid,
    conv_out,
    cotangent,
):
    core = lax.axis_index(CORE)
    chip = lax.axis_index(CHIPS)
    cell = lax.axis_index(CELL)
    chips = lax.axis_size(CHIPS)
    rows_here = velocity.shape[0]
    fields = jnp.stack([wave_now, wave_before, adjoint_last, adjoint_after]).reshape(
        4, 2, rows_here, 8, 128
    )
    kept = lax.dynamic_index_in_dim(fields, core, 1, keepdims=False)
    given = lax.dynamic_index_in_dim(fields, 1 - core, 1, keepdims=False)
    shared = jnp.concatenate(
        [velocity.reshape(rows_here, 8, 128), cotangent.reshape(rows_here // 8, 8, 128)]
    )
    mine = jnp.concatenate([kept.reshape(-1, 8, 128), shared])
    theirs = lax.ppermute(
        jnp.concatenate([given.reshape(-1, 8, 128), shared]), CORE, [(0, 1), (1, 0)]
    )
    lower = core == 0
    top = jnp.where(lower, mine, theirs)
    bottom = jnp.where(lower, theirs, mine)

    def joined(first, count):
        return [top[first : first + count], bottom[first : first + count]]

    r = rows_here
    waves = jnp.concatenate(joined(0, r) + joined(r, r))
    adjoints = jnp.concatenate(joined(2 * r, r) + joined(3 * r, r))
    velocity_chip = jnp.concatenate(joined(4 * r, r))
    cot_chip = jnp.concatenate(joined(5 * r, r // 8))
    up = [(i, i + 1) for i in range(chips - 1)]
    down = [(i + 1, i) for i in range(chips - 1)]
    low = lax.ppermute(jnp.concatenate([waves, velocity_chip, cot_chip[-1:]]), CHIPS, up)
    high = lax.ppermute(jnp.concatenate([waves, velocity_chip, cot_chip[:1]]), CHIPS, down)
    low_adjoint = lax.ppermute(adjoints, CHIPS, up)
    high_adjoint = lax.ppermute(adjoints, CHIPS, down)

    def of_shot(x):
        return lax.dynamic_index_in_dim(x, core, 0, keepdims=False)

    first_chip = (chip == 0).astype(jnp.float32)
    columns = jnp.arange(1024, dtype=jnp.int32)
    source = ((columns == of_shot(source_col)).astype(jnp.float32) * first_chip).reshape(8, 128)
    slots = jnp.arange(observed.shape[2], dtype=jnp.int32)
    begin, end, count = of_shot(rec_first), of_shot(rec_last), of_shot(rec_count)
    placed = begin + slots * (end - begin) // (count - 1)
    table = ((columns[:, None] == placed[None, :]) & (slots < count)[None, :]).astype(
        jnp.float32
    ) * first_chip
    counts = jnp.sum(table, axis=1).reshape(8, 128)
    recorded = jnp.einsum("tk,wk->tw", of_shot(observed), table, precision=highest).reshape(
        -1, 8, 128
    )

    stored, speeds = call(
        forward_kernel,
        [smem()] + [vmem()] * 5,
        (f32(STEPS, CHIP, 8, 128), f32(WIDE, 8, 128)),
        [scratch(2, WIDE, 8, 128)],
        of_shot(wavelet),
        source,
        low,
        waves,
        velocity_chip,
        high,
    )

    cot_around = jnp.concatenate(
        [low[-1], cot_chip.reshape(CHIP, 128), high[-1]], axis=0
    )
    cot_rows = jnp.pad(lax.dynamic_slice_in_dim(cot_around, 32 * core + 5, 38, 0), ((0, 2), (0, 0)))
    right_edge = cot_rows[1:37, 126:128].T
    left_edge = cot_rows[1:37, 0:2].T
    to_right = jnp.pad(right_edge, ((0, 6), (64, 28)))
    to_left = jnp.pad(left_edge, ((2, 4), (64, 28)))
    targets = jnp.arange(16, dtype=jnp.int32)
    target_cell = targets // 4 * 2 + targets % 2
    same_core = targets // 2 % 2 == core
    extra = (
        jnp.where((same_core & (target_cell == cell + 1))[:, None, None], to_right[None], 0.0)
        + jnp.where((same_core & (target_cell == cell - 1))[:, None, None], to_left[None], 0.0)
    )

    velocity_all = jnp.concatenate(
        [low[2 * CHIP + CHIP - 8 : 3 * CHIP], velocity_chip, high[2 * CHIP : 2 * CHIP + 8]], axis=0
    )
    velocity_rows = lax.dynamic_slice_in_dim(velocity_all, 32 * core + 5, 38, 0).reshape(38, 1024)
    velocity_wide = lax.dynamic_slice_in_dim(
        jnp.pad(velocity_rows, ((0, 2), (3, 253))), 128 * cell, 256, 1
    )
    velocity_wide = jnp.where(jnp.arange(256)[None, :] < 134, velocity_wide, 0.0)

    place = np.arange(FLAT)
    row_of, col_of = place // LINE, place % LINE
    own = (row_of >= 3) & (row_of < 35) & (col_of >= 3) & (col_of < 131)
    own = jnp.asarray(np.broadcast_to(own.astype(np.float32), (8, FLAT)))
    in_piece = (row_of < 38) & (col_of < 134)
    grid_row = jnp.asarray(row_of, jnp.int32) + (64 * chip + 32 * core - 3)
    grid_col = jnp.asarray(col_of, jnp.int32) + (128 * cell - 3)
    inside = (
        jnp.asarray(in_piece)
        & (grid_row >= 0)
        & (grid_row < 1024)
        & (grid_col >= 0)
        & (grid_col < 1024)
    )
    inside = jnp.broadcast_to(inside.astype(jnp.float32), (8, FLAT))

    first = jnp.pad(conv_in.reshape(CH, 9, 2), ((0, 0), (0, 1), (0, 6))).reshape(CH, 80)
    pulling = jnp.pad(
        conv_out.reshape(9, CH)[::-1].T[:, :, None], ((0, 0), (0, 1), (2, 5))
    ).reshape(CH, 80)
    first_high, first_low = stacked_weights(jnp.concatenate([first, pulling]))
    first_w = jnp.concatenate(
        [
            jnp.concatenate([first_high, first_high], axis=1),
            jnp.concatenate([first_low, jnp.zeros_like(first_low)], axis=1),
        ]
    )
    middle = conv_mid.reshape(CH, 9, CH)
    middle_w = three_terms(middle.transpose(1, 0, 2).reshape(9 * CH, CH))
    back_w = three_terms(middle.transpose(1, 2, 0).reshape(9 * CH, CH))
    last_w = three_terms(jnp.pad(conv_out.reshape(9, CH), ((0, 7), (0, 0))))

    pieces = call(
        adjoint_kernel,
        [vmem()] * 8,
        f32(16, 48, 128),
        [scratch(2, WIDE, 8, 128), scratch(CHIP * 8, 128), scratch(8, 128, 128)],
        counts,
        recorded,
        low_adjoint,
        adjoints,
        high_adjoint,
        speeds,
        stored,
        extra,
    )
    summed = jnp.sum(lax.all_to_all(pieces, SUMMED, 0, 0, tiled=True), axis=0)
    edge_rows = jnp.concatenate([jnp.where(lower, summed[0:8], summed[32:40]), summed[40:48]])
    bands = lax.axis_size(BAND)
    outward = [(b, b - 1) for b in range(2, bands, 2)] + [(b, b + 1) for b in range(1, bands - 1, 2)]
    arrived = lax.ppermute(edge_rows, BAND, outward)

    bf16 = jnp.bfloat16
    new_velocity, grads = call(
        network_kernel,
        [smem()] + [vmem()] * 10,
        (f32(32, 128), f32(CH, 512)),
        [
            scratch(8, FLAT + 2 * SIDE),
            scratch(160, FLAT, dtype=bf16),
            scratch(96, FLAT, dtype=bf16),
            scratch(CH, FLAT),
            scratch(CH, FLAT),
            scratch(9 * CH, FLAT + 2 * SIDE),
            scratch(16, FLAT + 2 * SIDE),
            scratch(CH, FLAT),
            scratch(CH, FLAT + 2 * SIDE),
            scratch(CH, FLAT),
            scratch(96, FLAT, dtype=bf16),
            scratch(96, FLAT, dtype=bf16),
            scratch(128, FLAT, dtype=bf16),
            scratch(8, FLAT),
        ],
        core.reshape(1).astype(jnp.int32),
        summed,
        arrived,
        velocity_wide,
        cot_rows,
        inside,
        own,
        first_w,
        middle_w,
        back_w,
        last_w,
    )
    total = over_pairs(grads, CORE, [(0, 1)])
    total = over_fours(total, "shot", [(0, 1, 2, 3)])
    total = over_fours(total, ("band_0", "net"), [(0, 1, 2, 3)])
    total = over_fours(total, "band_1", [(0, 2, 4, 6), (1, 3, 5, 7)])
    total = over_pairs(total, "band_1", [(0, 1), (2, 3), (4, 5), (6, 7)])
    grad_mid = total[:, 0:288]
    outer = total[:, 384:456].reshape(CH, 9, 8)
    grad_in = outer[:, :, 0:2].reshape(CH, 18)
    grad_out = outer[:, ::-1, 2].T.reshape(1, 9 * CH)
    return new_velocity, grad_in, grad_mid, grad_out


def solution(mesh):
    split_mesh = Mesh(
        mesh.devices.reshape(mesh.shape["shot"], 2, 8, 2, mesh.shape["net"]),
        ("shot", "band_0", "band_1", "band_2", "net"),
    )
    placed = (
        P(BAND, None),
        P(CELL, BAND, None),
        P(CELL, BAND, None),
        P(CELL, BAND, None),
        P(CELL, BAND, None),
        P(CELL, None),
        P(CELL),
        P(CELL),
        P(CELL),
        P(CELL),
        P(CELL, None, None),
        P(),
        P(),
        P(),
        P(BAND, CELL),
    )
    return jax.shard_map(
        on_device,
        mesh=split_mesh,
        in_specs=placed,
        out_specs=(P(BAND, CELL), P(), P(), P()),
        check_vma=False,
    )
```

```python
import numpy as np

import jax
import jax.numpy as jnp
from jax import lax
from jax.experimental import pallas as pl
from jax.experimental.pallas import tpu as pltpu
from jax.sharding import Mesh
from jax.sharding import PartitionSpec as P

BAND = ("band_0", "band_1", "band_2")
CHIPS = ("band_0", "band_1")
CORE = "band_2"
CELL = ("shot", "net")
SUMMED = ("shot", "band_2", "net")

coefficients = (-205.0 / 72.0, 8.0 / 5.0, -1.0 / 5.0, 8.0 / 315.0, -1.0 / 560.0)
speed_factor = 0.11
source_depth = 2
receiver_depth = 3
highest = lax.Precision.HIGHEST

STEPS = 16
CHIP = 64
BLOCK = 32
WAVES = 98
WIDE = 3 * CHIP
LINE = 136
FLAT = 42 * 128
PART = 768
SIDE = 256
CH = 32
vmem_limit = 56 * 1024 * 1024
TAPS = [(down - 1) * LINE + (across - 1) for down in range(3) for across in range(3)]


def stencil_constants():
    lane = lax.broadcasted_iota(jnp.int32, (8, 128), 1)
    column = lax.broadcasted_iota(jnp.int32, (8, 128), 0) * 128 + lane
    c0, c1, c2, c3, c4 = coefficients

    def where(mask, value):
        return jnp.where(mask, jnp.float32(value), jnp.float32(0.0))

    return dict(
        low1=lane < 1,
        low3=lane < 3,
        high1=lane >= 127,
        high3=lane >= 125,
        c1u=where(column != 0, c1),
        c1v=where(column != 1023, c1),
        c2p=where((column != 1021) & (column != 1022), c2),
        c3p=where(column <= 1020, c3),
        c4p=where((column <= 1020) & (column != 0), c4),
        c2m=where((column != 1) & (column != 2), c2),
        c3m=where(column >= 3, c3),
        c4m=where((column >= 3) & (column != 1023), c4),
    )


def from_left(x, count, mask):
    turned = pltpu.roll(x, count, 1)
    return jnp.where(mask, pltpu.roll(turned, 1, 0), turned)


def from_right(x, count, mask):
    turned = pltpu.roll(x, 128 - count, 1)
    return jnp.where(mask, pltpu.roll(turned, 7, 0), turned)


def advance(k, fields, speeds, now, step):
    other = 1 - now
    c0, c1, c2, c3, c4 = coefficients

    def block(first, count):
        rows = [fields[now, first - 4 + i] for i in range(count + 8)]
        prior = [fields[other, first + i] for i in range(count)]
        speed = [speeds[first + i] for i in range(count)]
        middle = rows[4 : 4 + count]
        left = [from_left(x, 1, k["low1"]) for x in middle]
        right = [from_right(x, 1, k["high1"]) for x in middle]
        ahead = [
            k["c2p"] * right[i] + k["c3p"] * middle[i] + k["c4p"] * left[i] for i in range(count)
        ]
        behind = [
            k["c2m"] * left[i] + k["c3m"] * middle[i] + k["c4m"] * right[i] for i in range(count)
        ]
        ahead = [from_left(x, 3, k["low3"]) for x in ahead]
        behind = [from_right(x, 3, k["high3"]) for x in behind]
        fresh = []
        for i in range(count):
            total = k["c1u"] * left[i] + k["c1v"] * right[i] + (2.0 * c0) * middle[i]
            for reach, weight in ((1, c1), (2, c2), (3, c3), (4, c4)):
                total = total + weight * (rows[i + 4 - reach] + rows[i + 4 + reach])
            total = total + (ahead[i] + behind[i])
            fresh.append((middle[i] + middle[i]) - prior[i] + speed[i] * total)
        for i in range(count):
            fields[other, first + i] = fresh[i]

    first, count = 4 * step, WIDE - 8 * step
    whole = count // BLOCK

    def body(i, carry):
        block(first + BLOCK * i, BLOCK)
        return carry

    lax.fori_loop(0, whole, body, 0)
    if count % BLOCK:
        block(first + BLOCK * whole, count % BLOCK)


def place_rows(core, pack, stride, put):
    for part in range(2):
        band = core if part == 0 else 1 - core

        def copy(i, carry, part=part, band=band):
            put(32 * band + 8 * i, lambda at: pack[pl.ds(stride * part + at + 8 * i, 8)])
            return carry

        lax.fori_loop(0, 4, copy, 0)


def forward_kernel(
    core_ref, pulses, source, low, mid, high, stored, speeds, velocity_rows, fields, velocity
):
    core = core_ref[0]
    for place, pack in ((0, low), (CHIP, mid), (2 * CHIP, high)):

        def put(row, rows_at, place=place):
            fields[0, pl.ds(place + row, 8)] = rows_at(0)
            fields[1, pl.ds(place + row, 8)] = rows_at(32)
            values = rows_at(64)
            velocity[pl.ds(place + row, 8)] = values
            scaled = values * speed_factor
            speeds[pl.ds(place + row, 8)] = scaled * scaled

        place_rows(core, pack, WAVES, put)
    for i in range(5):
        velocity_rows[8 * i : 8 * i + 8] = velocity[pl.ds(CHIP - 3 + 32 * core + 8 * i, 8)]
    k = stencil_constants()
    for n in range(STEPS):
        now = n % 2
        advance(k, fields, speeds, now, n + 1)
        row = CHIP + source_depth
        fields[1 - now, row] = fields[1 - now, row] + pulses[n] * source[...]

        def keep(i, carry, n=n, now=now):
            for part in range(2):
                at = 8 * (2 * i + part)
                stored[n, pl.ds(at, 8)] = fields[1 - now, pl.ds(CHIP + at, 8)]
            return carry

        lax.fori_loop(0, 4, keep, 0)


def adjoint_kernel(core_ref, counts, recorded, low, mid, high, speeds, stored, extra, out, fields, image3, turned):
    core = core_ref[0]
    for place, pack in ((0, low), (CHIP, mid), (2 * CHIP, high)):

        def put(row, rows_at, place=place):
            fields[0, pl.ds(place + row, 8)] = rows_at(0)
            fields[1, pl.ds(place + row, 8)] = rows_at(32)

        place_rows(core, pack, CHIP, put)
    k = stencil_constants()
    for m in range(STEPS):
        now = m % 2
        n = STEPS - 1 - m
        advance(k, fields, speeds, now, m + 1)
        row = CHIP + receiver_depth
        push = counts[...] * stored[n, receiver_depth] - recorded[n]
        fields[1 - now, row] = fields[1 - now, row] + push

        def add(i, carry, n=n, m=m, now=now):
            for part in range(2):
                at = 8 * (2 * i + part)
                product = stored[n, pl.ds(at, 8)] * fields[1 - now, pl.ds(CHIP + at, 8)]
                if m:
                    product = image3[pl.ds(at, 8)] + product
                image3[pl.ds(at, 8)] = product
            return carry

        lax.fori_loop(0, 4, add, 0)
    image = image3.reshape(CHIP * 8, 128)
    blank = jnp.zeros((64, 128), jnp.float32)
    for j in range(8):
        block = jnp.concatenate(
            [image[pl.ds(64 * b + j, 8, stride=8), :] for b in range(8)], axis=0
        )
        for half in range(2):
            d = ((j // 2) * 2 + half) * 2 + j % 2
            out[d, 0:40, :] = block[24 * half : 24 * half + 40]
        turned[j] = jnp.transpose(jnp.concatenate([block, blank], axis=0))
    sub = lax.broadcasted_iota(jnp.int32, (8, 128), 0)
    for j in range(8):
        edges = jnp.zeros((8, 128), jnp.float32)
        if j > 0:
            edges = jnp.where(sub < 3, pltpu.roll(turned[j - 1, 120:128, :], 3, 0), edges)
        if j < 7:
            edges = jnp.where(
                (sub >= 3) & (sub < 6), pltpu.roll(turned[j + 1, 0:8, :], 3, 0), edges
            )
        for half in range(2):
            d = ((j // 2) * 2 + half) * 2 + j % 2
            out[d, 40:48, :] = edges + extra[d]


def pack_kernel(core_ref, now, before, last, after, velocity, cotangent, mine, given):
    core = core_ref[0]
    for which, out in ((core, mine), (1 - core, given)):
        for ref, first in ((now, 0), (before, 32), (velocity, 64), (last, WAVES), (after, WAVES + 32)):
            for b in range(4):
                for s in range(8):
                    rows, lanes = slice(8 * b, 8 * b + 8), slice(128 * s, 128 * s + 128)
                    tile = ref[rows, lanes] if ref is velocity else ref[which, rows, lanes]
                    out[pl.ds(8 * (first + 8 * b) + s, 8, stride=8), :] = tile
        for b, at in ((0, WAVES - 2), (3, WAVES - 1), (1, WAVES + 64), (2, WAVES + 65)):
            out[8 * at : 8 * at + 8, :] = cotangent[8 * b : 8 * b + 8, :]


def split(x):
    high = x.astype(jnp.bfloat16)
    low = (x - high.astype(jnp.float32)).astype(jnp.bfloat16)
    return high, low


def window(ref, rows, first, count, shift):
    start = SIDE + first + shift
    base = start // 128 * 128
    offset = start - base
    if offset == 0:
        return ref[rows, base : base + count]
    wide = ref[rows, base : base + count + 128]
    return pltpu.roll(wide, count + 128 - offset, 1)[:, :count]


def mul(left, right):
    return jnp.dot(left, right, preferred_element_type=jnp.float32)


def mul_t(left, right):
    return lax.dot_general(
        left, right, (((1,), (1,)), ((), ())), preferred_element_type=jnp.float32
    )


def network_kernel(
    core, summed, arrived, velocity_wide, cotangent_rows, inside, own, first_w, middle_w, back_w, last_w,
    new_velocity, grads,
    base, taps, packed, slope_one_d, before, products, last_products, pairs, hidden_one, slope_own, packed_two, packed_slope, own_terms, updates,
):
    lane = lax.broadcasted_iota(jnp.int32, (8, 128), 1)
    sub = lax.broadcasted_iota(jnp.int32, (8, 128), 0)
    lower = core[0] == 0
    edges = summed[40:48, :]
    other_edges = arrived[8:16, :]
    edge_rows = jnp.where(
        lower,
        jnp.where(lane < 3, pltpu.roll(other_edges, 67, 1), pltpu.roll(edges, 3, 1)),
        jnp.where(
            (lane >= 35) & (lane < 38), pltpu.roll(other_edges, 35, 1), pltpu.roll(edges, 99, 1)
        ),
    )
    turned = jnp.transpose(
        jnp.concatenate(
            [edge_rows, pltpu.roll(edges, 65, 1), jnp.zeros((112, 128), jnp.float32)], axis=0
        )
    )[0:40]
    main = summed[0:40, :]
    tile = pltpu.roll(arrived[0:8, :], 3, 0)
    down = pltpu.roll(main, 3, 0)
    up = pltpu.roll(main, 35, 0)
    low_case = jnp.concatenate([jnp.where(sub < 3, tile, down[0:8]), down[8:40]], axis=0)
    high_case = jnp.concatenate(
        [up[0:32], jnp.where((sub >= 3) & (sub < 6), tile, up[32:40])], axis=0
    )
    image = jnp.where(lower, low_case, high_case)
    lanes = lax.broadcasted_iota(jnp.int32, (40, 128), 1)
    scale = 1.0 / float(STEPS * 16) ** 0.5
    shifted = pltpu.roll(image, 3, 1)
    image_a = jnp.where(lanes < 3, turned, shifted) * scale
    image_b = jnp.where(lanes < 3, shifted, jnp.where(lanes < 6, turned, 0.0)) * scale
    shifted = pltpu.roll(cotangent_rows[...], 3, 1)
    sides = pltpu.roll(turned, 121, 1)
    cot_a = jnp.where(lanes < 1, 0.0, jnp.where(lanes < 3, sides, shifted))
    cot_b = jnp.where(lanes < 3, shifted, jnp.where(lanes < 5, sides, 0.0))
    velocity_all = velocity_wide[...]

    base[...] = jnp.zeros(base.shape, jnp.float32)
    wide_rows = [
        velocity_all,
        jnp.concatenate([image_a, image_b], axis=1),
        jnp.concatenate([cot_a, cot_b], axis=1),
    ]
    for channel, wide in enumerate(wide_rows):
        pieces = {}
        for r in range(38):
            start = LINE * r
            v, offset = start // 128, start % 128
            row = wide[r : r + 1, :]
            if offset:
                row = pltpu.roll(row, offset, 1)
            pieces.setdefault(v, []).append(row[:, 0:128])
            pieces.setdefault(v + 1, []).append(row[:, 128:256])
        for v, found in pieces.items():
            total = found[0]
            for piece in found[1:]:
                total = total + piece
            base[channel : channel + 1, SIDE + 128 * v : SIDE + 128 * v + 128] = total

    parts = [(p * PART, slice(p * PART, (p + 1) * PART)) for p in range(FLAT // PART)]
    all_rows = slice(0, 8)
    padding = jnp.zeros((8, PART), jnp.float32)
    for first, cut in parts:
        gathered = [window(base, all_rows, first, PART, shift) for shift in TAPS]
        high, low = split(jnp.concatenate(gathered + [padding], axis=0))
        taps[0:80, cut] = high
        taps[80:160, cut] = low
        result = mul(first_w[...], taps[:, cut])
        result = result[0:64] + result[64:128]
        value = result[0:CH]
        pulled = jax.nn.sigmoid(value)
        slope_one_d[:, cut] = pulled * (1.0 + value * (1.0 - pulled))
        mask = inside[:, cut] > 0.0
        mask = jnp.concatenate([mask] * 4, axis=0)
        hidden = jnp.where(mask, value * pulled, 0.0)
        hidden_one[:, SIDE + first : SIDE + first + PART] = hidden
        before[:, cut] = result[CH : 2 * CH]
        high, low = split(hidden)
        packed[0:32, cut] = high
        packed[32:64, cut] = low
        packed[64:96, cut] = high
    edge = jnp.zeros((CH, SIDE), jnp.float32)
    hidden_one[:, 0:SIDE] = edge
    hidden_one[:, SIDE + FLAT :] = edge
    zero_edge = jnp.zeros((9 * CH, SIDE), jnp.float32)
    products[:, 0:SIDE] = zero_edge
    products[:, SIDE + FLAT :] = zero_edge
    last_products[:, 0:SIDE] = jnp.zeros((16, SIDE), jnp.float32)
    last_products[:, SIDE + FLAT :] = jnp.zeros((16, SIDE), jnp.float32)

    for first, cut in parts:
        products[:, SIDE + first : SIDE + first + PART] = mul(middle_w[...], packed[:, cut])
    for first, cut in parts:
        mask = inside[:, cut] > 0.0
        here = own[:, cut] > 0.0
        for g in range(4):
            total = None
            for tap, shift in enumerate(TAPS):
                piece = window(
                    products, slice(tap * CH + 8 * g, tap * CH + 8 * g + 8), first, PART, shift
                )
                total = piece if total is None else total + piece
            pulled = jax.nn.sigmoid(total)
            rows = slice(8 * g, 8 * g + 8)
            hidden = jnp.where(mask, total * pulled, 0.0)
            slope = jnp.where(
                mask, before[rows, cut] * (pulled * (1.0 + total * (1.0 - pulled))), 0.0
            )
            pairs[rows, cut] = hidden
            slope_own[rows, cut] = slope
        hidden = pairs[:, cut]
        slope = slope_own[:, cut]
        high, low = split(hidden)
        packed_two[0:32, cut] = high
        packed_two[32:64, cut] = low
        packed_two[64:96, cut] = high
        here = jnp.concatenate([here] * 4, axis=0)
        high, low = split(jnp.where(here, hidden, 0.0))
        own_terms[32:64, cut] = high
        own_terms[96:128, cut] = low
        high, low = split(slope)
        packed_slope[0:32, cut] = high
        packed_slope[32:64, cut] = low
        packed_slope[64:96, cut] = high
        last_products[:, SIDE + first : SIDE + first + PART] = mul(last_w[...], packed_two[:, cut])

    wide_sub = lax.broadcasted_iota(jnp.int32, (8, PART), 0)
    for first, cut in parts:
        total = jnp.zeros((8, PART), jnp.float32)
        for tap, shift in enumerate(TAPS):
            rows = slice(0, 8) if tap < 8 else slice(8, 16)
            piece = window(last_products, rows, first, PART, shift)
            total = total + jnp.where(wide_sub == tap % 8, piece, 0.0)
        updates[0:1, cut] = jnp.sum(total, axis=0, keepdims=True)
    velocity_here = pltpu.roll(velocity_all, 253, 1)[:, 0:128]
    for r in range(32):
        start = LINE * (r + 3) + 3
        v, offset = start // 128, start % 128
        row = updates[0:1, 128 * v : 128 * v + 256]
        if offset:
            row = pltpu.roll(row, 256 - offset, 1)
        new_velocity[r : r + 1, :] = velocity_here[r + 3 : r + 4] + row[:, 0:128]

    for first, cut in parts:
        products[:, SIDE + first : SIDE + first + PART] = mul(back_w[...], packed_slope[:, cut])
    for first, cut in parts:
        here = own[:, cut] > 0.0
        for g in range(4):
            total = None
            for tap, shift in enumerate(TAPS):
                piece = window(
                    products, slice(tap * CH + 8 * g, tap * CH + 8 * g + 8), first, PART, -shift
                )
                total = piece if total is None else total + piece
            rows = slice(8 * g, 8 * g + 8)
            pairs[rows, cut] = jnp.where(here, total * slope_one_d[rows, cut], 0.0)
        high, low = split(pairs[:, cut])
        own_terms[0:32, cut] = high
        own_terms[64:96, cut] = low

    middle_sum = jnp.zeros((CH, 9 * CH), jnp.float32)
    outer_sum = jnp.zeros((64, 80), jnp.float32)
    for first, cut in parts:
        here = jnp.concatenate([own[:, cut] > 0.0] * 4, axis=0)
        shifted = jnp.concatenate(
            [window(hidden_one, slice(0, CH), first, PART, shift) for shift in TAPS], axis=0
        )
        high, low = split(shifted)
        slope_high, slope_low = split(jnp.where(here, slope_own[:, cut], 0.0))
        both = mul_t(jnp.concatenate([slope_high, slope_low], axis=0), high)
        middle_sum = middle_sum + (both[0:CH] + both[CH:] + mul_t(slope_high, low))
        terms = own_terms[:, cut]
        both = mul_t(terms, taps[0:80, cut])
        outer_sum = outer_sum + (both[0:64] + both[64:128] + mul_t(terms[0:64], taps[80:160, cut]))
    column = lax.broadcasted_iota(jnp.int32, (CH, 80), 1)
    mixed = jnp.where(column % 8 < 2, outer_sum[0:CH], outer_sum[CH:64])
    mixed = pltpu.roll(jnp.concatenate([mixed, jnp.zeros((CH, 48), jnp.float32)], axis=1), 32, 1)
    grads[:, 0:256] = middle_sum[:, 0:256]
    tail = jnp.concatenate([middle_sum[:, 256:288], jnp.zeros((CH, 96), jnp.float32)], axis=1)
    grads[:, 256:384] = tail + mixed


def vmem():
    return pl.BlockSpec(memory_space=pltpu.VMEM)


def smem():
    return pl.BlockSpec(memory_space=pltpu.SMEM)


def f32(*shape):
    return jax.ShapeDtypeStruct(shape, jnp.float32)


def scratch(*shape, dtype=jnp.float32):
    return pltpu.VMEM(shape, dtype)


def call(kernel, in_specs, out_shape, scratch_shapes, *operands):
    many = isinstance(out_shape, tuple)
    return pl.pallas_call(
        kernel,
        in_specs=in_specs,
        out_specs=tuple(vmem() for _ in out_shape) if many else vmem(),
        out_shape=out_shape,
        scratch_shapes=scratch_shapes,
        compiler_params=pltpu.CompilerParams(vmem_limit_bytes=vmem_limit),
    )(*operands)


def stacked_weights(weights):
    high = weights.astype(jnp.bfloat16)
    low = (weights - lax.reduce_precision(weights, 8, 7)).astype(jnp.bfloat16)
    return high, low


def three_terms(weights):
    high, low = stacked_weights(weights)
    return jnp.concatenate([high, high, low], axis=1)


def over_pairs(x, axis, groups):
    return x + lax.ppermute(x, axis, [(a, b) for a, b in groups] + [(b, a) for a, b in groups])


def over_fours(x, axis, groups):
    near, far, cross = (
        lax.ppermute(x, axis, [(group[i], group[i ^ turn]) for group in groups for i in range(4)])
        for turn in (1, 2, 3)
    )
    return (x + near) + (far + cross)


def on_device(
    velocity,
    wave_now,
    wave_before,
    adjoint_last,
    adjoint_after,
    wavelet,
    source_col,
    rec_first,
    rec_last,
    rec_count,
    observed,
    conv_in,
    conv_mid,
    conv_out,
    cotangent,
):
    core = lax.axis_index(CORE)
    chip = lax.axis_index(CHIPS)
    cell = lax.axis_index(CELL)
    chips = lax.axis_size(CHIPS)
    core_id = core.reshape(1).astype(jnp.int32)
    packed_rows = WAVES + 66
    mine, given = call(
        pack_kernel,
        [smem()] + [vmem()] * 6,
        (f32(packed_rows * 8, 128), f32(packed_rows * 8, 128)),
        [],
        core_id,
        wave_now,
        wave_before,
        adjoint_last,
        adjoint_after,
        velocity,
        cotangent,
    )
    mine = mine.reshape(packed_rows, 8, 128)
    theirs = lax.ppermute(given.reshape(packed_rows, 8, 128), CORE, [(0, 1), (1, 0)])
    waves = jnp.concatenate([mine[:WAVES], theirs[:WAVES]])
    up = [(i, i + 1) for i in range(chips - 1)]
    down = [(i + 1, i) for i in range(chips - 1)]
    low = lax.ppermute(waves, CHIPS, up)
    high = lax.ppermute(waves, CHIPS, down)
    (
        mine, theirs, wavelet, source_col, rec_first, rec_last, rec_count, observed, conv_in, conv_mid, conv_out, core, chip, cell,
    ) = lax.optimization_barrier(
        (
            mine, theirs, wavelet, source_col, rec_first, rec_last, rec_count, observed, conv_in, conv_mid, conv_out, core, chip, cell,
        )
    )
    lower = core == 0

    def of_shot(x):
        return lax.dynamic_index_in_dim(x, core, 0, keepdims=False)

    first_chip = (chip == 0).astype(jnp.float32)
    columns = jnp.arange(1024, dtype=jnp.int32)
    source = ((columns == of_shot(source_col)).astype(jnp.float32) * first_chip).reshape(8, 128)
    slots = jnp.arange(observed.shape[2], dtype=jnp.int32)
    begin, end, count = of_shot(rec_first), of_shot(rec_last), of_shot(rec_count)
    placed = begin + slots * (end - begin) // (count - 1)
    table = ((columns[:, None] == placed[None, :]) & (slots < count)[None, :]).astype(
        jnp.float32
    ) * first_chip
    counts = jnp.sum(table, axis=1).reshape(8, 128)
    recorded = jnp.einsum("tk,wk->tw", of_shot(observed), table, precision=highest).reshape(
        -1, 8, 128
    )

    adjoints = jnp.concatenate([mine[WAVES : WAVES + 64], theirs[WAVES : WAVES + 64]])
    adjoints, counts, recorded, source = lax.optimization_barrier(
        (adjoints, counts, recorded, source)
    )
    low_adjoint = lax.ppermute(adjoints, CHIPS, up)
    high_adjoint = lax.ppermute(adjoints, CHIPS, down)

    stored, speeds, velocity_rows = call(
        forward_kernel,
        [smem()] * 2 + [vmem()] * 4,
        (f32(STEPS, CHIP, 8, 128), f32(WIDE, 8, 128), f32(40, 8, 128)),
        [scratch(2, WIDE, 8, 128), scratch(WIDE, 8, 128)],
        core_id,
        of_shot(wavelet),
        source,
        low,
        waves,
        high,
    )

    def cot_of(pack):
        return [pack[WAVES - 2], pack[WAVES + 64], pack[WAVES + 65], pack[WAVES - 1]]

    cot_mine = jnp.concatenate(cot_of(mine))
    cot_theirs = jnp.concatenate(cot_of(theirs))
    cot_before = jnp.where(lower, low[2 * WAVES - 1], low[WAVES - 1])
    cot_after = jnp.where(lower, high[WAVES - 2], high[2 * WAVES - 2])
    cot_around = jnp.concatenate(
        [
            cot_before,
            jnp.where(lower, cot_mine, cot_theirs),
            jnp.where(lower, cot_theirs, cot_mine),
            cot_after,
        ]
    )
    cot_rows = jnp.pad(lax.dynamic_slice_in_dim(cot_around, 32 * core + 5, 38, 0), ((0, 2), (0, 0)))
    right_edge = cot_rows[1:37, 126:128].T
    left_edge = cot_rows[1:37, 0:2].T
    to_right = jnp.pad(right_edge, ((0, 6), (64, 28)))
    to_left = jnp.pad(left_edge, ((2, 4), (64, 28)))
    targets = jnp.arange(16, dtype=jnp.int32)
    target_cell = targets // 4 * 2 + targets % 2
    same_core = targets // 2 % 2 == core
    extra = (
        jnp.where((same_core & (target_cell == cell + 1))[:, None, None], to_right[None], 0.0)
        + jnp.where((same_core & (target_cell == cell - 1))[:, None, None], to_left[None], 0.0)
    )

    velocity_wide = lax.dynamic_slice_in_dim(
        jnp.pad(velocity_rows.reshape(40, 1024), ((0, 0), (3, 253))), 128 * cell, 256, 1
    )
    velocity_wide = jnp.where(jnp.arange(256)[None, :] < 134, velocity_wide, 0.0)

    place = np.arange(FLAT)
    row_of, col_of = place // LINE, place % LINE
    own = (row_of >= 3) & (row_of < 35) & (col_of >= 3) & (col_of < 131)
    own = jnp.asarray(np.broadcast_to(own.astype(np.float32), (8, FLAT)))
    in_piece = (row_of < 38) & (col_of < 134)
    grid_row = jnp.asarray(row_of, jnp.int32) + (64 * chip + 32 * core - 3)
    grid_col = jnp.asarray(col_of, jnp.int32) + (128 * cell - 3)
    inside = (
        jnp.asarray(in_piece)
        & (grid_row >= 0)
        & (grid_row < 1024)
        & (grid_col >= 0)
        & (grid_col < 1024)
    )
    inside = jnp.broadcast_to(inside.astype(jnp.float32), (8, FLAT))

    first = jnp.pad(conv_in.reshape(CH, 9, 2), ((0, 0), (0, 1), (0, 6))).reshape(CH, 80)
    pulling = jnp.pad(
        conv_out.reshape(9, CH)[::-1].T[:, :, None], ((0, 0), (0, 1), (2, 5))
    ).reshape(CH, 80)
    first_high, first_low = stacked_weights(jnp.concatenate([first, pulling]))
    first_w = jnp.concatenate(
        [
            jnp.concatenate([first_high, first_high], axis=1),
            jnp.concatenate([first_low, jnp.zeros_like(first_low)], axis=1),
        ]
    )
    middle = conv_mid.reshape(CH, 9, CH)
    middle_w = three_terms(middle.transpose(1, 0, 2).reshape(9 * CH, CH))
    back_w = three_terms(middle.transpose(1, 2, 0).reshape(9 * CH, CH))
    last_w = three_terms(jnp.pad(conv_out.reshape(9, CH), ((0, 7), (0, 0))))

    pieces = call(
        adjoint_kernel,
        [smem()] + [vmem()] * 8,
        f32(16, 48, 128),
        [scratch(2, WIDE, 8, 128), scratch(CHIP, 8, 128), scratch(8, 128, 128)],
        core_id,
        counts,
        recorded,
        low_adjoint,
        adjoints,
        high_adjoint,
        speeds,
        stored,
        extra,
    )
    summed = jnp.sum(lax.all_to_all(pieces, SUMMED, 0, 0, tiled=True), axis=0)
    edge_rows = jnp.concatenate([jnp.where(lower, summed[0:8], summed[32:40]), summed[40:48]])
    bands = lax.axis_size(BAND)
    outward = [(b, b - 1) for b in range(2, bands, 2)] + [(b, b + 1) for b in range(1, bands - 1, 2)]
    arrived = lax.ppermute(edge_rows, BAND, outward)

    bf16 = jnp.bfloat16
    new_velocity, grads = call(
        network_kernel,
        [smem()] + [vmem()] * 10,
        (f32(32, 128), f32(CH, 384)),
        [
            scratch(8, FLAT + 2 * SIDE),
            scratch(160, FLAT, dtype=bf16),
            scratch(96, FLAT, dtype=bf16),
            scratch(CH, FLAT),
            scratch(CH, FLAT),
            scratch(9 * CH, FLAT + 2 * SIDE),
            scratch(16, FLAT + 2 * SIDE),
            scratch(CH, FLAT),
            scratch(CH, FLAT + 2 * SIDE),
            scratch(CH, FLAT),
            scratch(96, FLAT, dtype=bf16),
            scratch(96, FLAT, dtype=bf16),
            scratch(128, FLAT, dtype=bf16),
            scratch(8, FLAT),
        ],
        core_id,
        summed,
        arrived,
        velocity_wide,
        cot_rows,
        inside,
        own,
        first_w,
        middle_w,
        back_w,
        last_w,
    )
    total = over_pairs(grads, CORE, [(0, 1)])
    total = over_fours(total, "shot", [(0, 1, 2, 3)])
    total = over_fours(total, ("band_0", "net"), [(0, 1, 2, 3)])
    total = over_fours(total, "band_1", [(0, 2, 4, 6), (1, 3, 5, 7)])
    total = over_pairs(total, "band_1", [(0, 1), (2, 3), (4, 5), (6, 7)])
    grad_mid = total[:, 0:288]
    outer = total[:, 288:360].reshape(CH, 9, 8)
    grad_in = outer[:, :, 0:2].reshape(CH, 18)
    grad_out = outer[:, ::-1, 2].T.reshape(1, 9 * CH)
    return new_velocity, grad_in, grad_mid, grad_out


def solution(mesh):
    split_mesh = Mesh(
        mesh.devices.reshape(mesh.shape["shot"], 2, 8, 2, mesh.shape["net"]),
        ("shot", "band_0", "band_1", "band_2", "net"),
    )
    placed = (
        P(BAND, None),
        P(CELL, BAND, None),
        P(CELL, BAND, None),
        P(CELL, BAND, None),
        P(CELL, BAND, None),
        P(CELL, None),
        P(CELL),
        P(CELL),
        P(CELL),
        P(CELL),
        P(CELL, None, None),
        P(),
        P(),
        P(),
        P(BAND, CELL),
    )
    return jax.shard_map(
        on_device,
        mesh=split_mesh,
        in_specs=placed,
        out_specs=(P(BAND, CELL), P(), P(), P()),
        check_vma=False,
    )
```

```python
import jax
import jax.numpy as jnp
from jax import lax
from jax.experimental import pallas as pl
from jax.experimental.pallas import tpu as pltpu
from jax.sharding import Mesh
from jax.sharding import PartitionSpec as P

BAND = ("band_0", "band_1", "band_2")
CHIPS = ("band_0", "band_1")
CORE = "band_2"
CELL = ("shot", "net")
SUMMED = ("shot", "band_2", "net")

coefficients = (-205.0 / 72.0, 8.0 / 5.0, -1.0 / 5.0, 8.0 / 315.0, -1.0 / 560.0)
speed_factor = 0.11
source_depth = 2
receiver_depth = 3
highest = lax.Precision.HIGHEST

STEPS = 16
CHIP = 64
BLOCK = 64
WAVES = 100
WIDE = 3 * CHIP
LINE = 136
FLAT = 42 * 128
PART = 768
SIDE = 256
CH = 32
vmem_limit = 56 * 1024 * 1024
TAPS = [(down - 1) * LINE + (across - 1) for down in range(3) for across in range(3)]


def stencil_constants():
    lane = lax.broadcasted_iota(jnp.int32, (8, 128), 1)
    column = lax.broadcasted_iota(jnp.int32, (8, 128), 0) * 128 + lane
    c0, c1, c2, c3, c4 = coefficients

    def where(mask, value):
        return jnp.where(mask, jnp.float32(value), jnp.float32(0.0))

    return dict(
        low1=lane < 1,
        low3=lane < 3,
        high1=lane >= 127,
        high3=lane >= 125,
        c1u=where(column != 0, c1),
        c1v=where(column != 1023, c1),
        c2p=where((column != 1021) & (column != 1022), c2),
        c3p=where(column <= 1020, c3),
        c4p=where((column <= 1020) & (column != 0), c4),
        c2m=where((column != 1) & (column != 2), c2),
        c3m=where(column >= 3, c3),
        c4m=where((column >= 3) & (column != 1023), c4),
    )


def from_left(x, count, mask):
    turned = pltpu.roll(x, count, 1)
    return jnp.where(mask, pltpu.roll(turned, 1, 0), turned)


def from_right(x, count, mask):
    turned = pltpu.roll(x, 128 - count, 1)
    return jnp.where(mask, pltpu.roll(turned, 7, 0), turned)


def advance(k, fields, speeds, now, step):
    other = 1 - now
    c0, c1, c2, c3, c4 = coefficients

    def block(first, count):
        rows = [fields[now, first - 4 + i] for i in range(count + 8)]
        prior = [fields[other, first + i] for i in range(count)]
        speed = [speeds[first + i] for i in range(count)]
        middle = rows[4 : 4 + count]
        left = [from_left(x, 1, k["low1"]) for x in middle]
        right = [from_right(x, 1, k["high1"]) for x in middle]
        ahead = [
            k["c2p"] * right[i] + k["c3p"] * middle[i] + k["c4p"] * left[i] for i in range(count)
        ]
        behind = [
            k["c2m"] * left[i] + k["c3m"] * middle[i] + k["c4m"] * right[i] for i in range(count)
        ]
        ahead = [from_left(x, 3, k["low3"]) for x in ahead]
        behind = [from_right(x, 3, k["high3"]) for x in behind]
        fresh = []
        for i in range(count):
            total = k["c1u"] * left[i] + k["c1v"] * right[i] + (2.0 * c0) * middle[i]
            for reach, weight in ((1, c1), (2, c2), (3, c3), (4, c4)):
                total = total + weight * (rows[i + 4 - reach] + rows[i + 4 + reach])
            total = total + (ahead[i] + behind[i])
            fresh.append((middle[i] + middle[i]) - prior[i] + speed[i] * total)
        for i in range(count):
            fields[other, first + i] = fresh[i]

    first, count = 4 * step, WIDE - 8 * step
    whole = count // BLOCK

    def body(i, carry):
        block(first + BLOCK * i, BLOCK)
        return carry

    lax.fori_loop(0, whole, body, 0)
    if count % BLOCK:
        block(first + BLOCK * whole, count % BLOCK)


def band_copies(core, packs, stride, targets, sems):
    copies = []
    for place, pack in zip((0, CHIP, 2 * CHIP), packs):
        for part in range(2):
            band = core if part == 0 else 1 - core
            for i, target in enumerate(targets):
                copies.append(
                    pltpu.make_async_copy(
                        pack.at[pl.ds(stride * part + 32 * i, 32)],
                        target.at[pl.ds(place + 32 * band, 32)],
                        sems.at[len(copies)],
                    )
                )
    return copies


def forward_kernel(
    core_ref, pulses, source, low, mid, high,
    stored, speeds, velocity_rows, cot_rows,
    fields, velocity, cot, sems, cot_sems, out_sems,
):
    core = core_ref[0]
    copies = band_copies(core, (low, mid, high), WAVES, (fields.at[0], fields.at[1], velocity), sems)
    cot_copies = [
        pltpu.make_async_copy(low.at[WAVES * (1 - core) + 99], cot.at[0], cot_sems.at[0]),
        pltpu.make_async_copy(
            mid.at[pl.ds(96, 4)], cot.at[pl.ds(1 + 4 * core, 4)], cot_sems.at[1]
        ),
        pltpu.make_async_copy(
            mid.at[pl.ds(WAVES + 96, 4)], cot.at[pl.ds(5 - 4 * core, 4)], cot_sems.at[2]
        ),
        pltpu.make_async_copy(high.at[WAVES * core + 96], cot.at[9], cot_sems.at[3]),
    ]
    for copy in copies + cot_copies:
        copy.start()
    for copy in copies + cot_copies:
        copy.wait()

    def square(i, carry):
        at = pl.ds(8 * i, 8)
        scaled = velocity[at] * speed_factor
        speeds[at] = scaled * scaled
        return carry

    lax.fori_loop(0, WIDE // 8, square, 0)
    for i in range(5):
        velocity_rows[8 * i : 8 * i + 8] = velocity[pl.ds(CHIP - 3 + 32 * core + 8 * i, 8)]
    tiles = cot[pl.ds(4 * core, 6)].reshape(48, 128)
    cot_rows[...] = pltpu.roll(tiles, 43, 0)[0:40]
    k = stencil_constants()
    saves = []
    for n in range(STEPS):
        now = n % 2
        if n >= 2:
            saves[n - 2].wait()
        advance(k, fields, speeds, now, n + 1)
        row = CHIP + source_depth
        fields[1 - now, row] = fields[1 - now, row] + pulses[core, n] * source[...]
        saves.append(
            pltpu.make_async_copy(
                fields.at[1 - now, pl.ds(CHIP, CHIP)], stored.at[n], out_sems.at[n % 2]
            )
        )
        saves[n].start()
    saves[STEPS - 2].wait()
    saves[STEPS - 1].wait()


def adjoint_kernel(
    core_ref, cell_ref, counts, recorded, low, mid, high, speeds, stored, cot_rows,
    out,
    fields, image3, turned, passed, sems, in_sems,
):
    core = core_ref[0]
    cell = cell_ref[0]
    copies = band_copies(core, (low, mid, high), CHIP, (fields.at[0], fields.at[1]), sems)
    loads = [
        pltpu.make_async_copy(stored.at[n], passed.at[n % 2], in_sems.at[n % 2])
        for n in range(STEPS)
    ]
    loads[STEPS - 1].start()
    for copy in copies:
        copy.start()
    for copy in copies:
        copy.wait()
    k = stencil_constants()
    for m in range(STEPS):
        now = m % 2
        n = STEPS - 1 - m
        loads[n].wait()
        if n:
            loads[n - 1].start()
        advance(k, fields, speeds, now, m + 1)
        row = CHIP + receiver_depth
        push = counts[...] * passed[n % 2, receiver_depth] - recorded[n]
        fields[1 - now, row] = fields[1 - now, row] + push

        for at in range(0, CHIP, 8):
            product = passed[n % 2, at : at + 8] * fields[1 - now, CHIP + at : CHIP + at + 8]
            if m:
                product = image3[at : at + 8] + product
            image3[at : at + 8] = product
    image = image3.reshape(CHIP * 8, 128)
    blank = jnp.zeros((64, 128), jnp.float32)
    for j in range(8):
        block = jnp.concatenate(
            [image[pl.ds(64 * b + j, 8, stride=8), :] for b in range(8)], axis=0
        )
        for half in range(2):
            d = ((j // 2) * 2 + half) * 2 + j % 2
            out[d, 0:40, :] = block[24 * half : 24 * half + 40]
        turned[j] = jnp.transpose(jnp.concatenate([block, blank], axis=0))
    sub = lax.broadcasted_iota(jnp.int32, (8, 128), 0)
    lane = lax.broadcasted_iota(jnp.int32, (8, 128), 1)
    columns = jnp.transpose(
        jnp.concatenate([cot_rows[...], jnp.zeros((88, 128), jnp.float32)], axis=0)
    )
    here = (lane >= 64) & (lane < 100)
    to_right = pltpu.roll(pltpu.roll(columns[120:128], 2, 0), 63, 1)
    to_right = jnp.where(here & (sub < 2), to_right, 0.0)
    to_left = pltpu.roll(pltpu.roll(columns[0:8], 2, 0), 63, 1)
    to_left = jnp.where(here & (sub >= 2) & (sub < 4), to_left, 0.0)
    for j in range(8):
        edges = jnp.zeros((8, 128), jnp.float32)
        if j > 0:
            edges = jnp.where(sub < 3, pltpu.roll(turned[j - 1, 120:128, :], 3, 0), edges)
        if j < 7:
            edges = jnp.where(
                (sub >= 3) & (sub < 6), pltpu.roll(turned[j + 1, 0:8, :], 3, 0), edges
            )
        for half in range(2):
            d = ((j // 2) * 2 + half) * 2 + j % 2
            extra = jnp.where((cell == j - 1) & (core == half), to_right, 0.0)
            extra = jnp.where((cell == j + 1) & (core == half), to_left, extra)
            out[d, 40:48, :] = edges + extra


def pack_rows(which, refs, out):
    for place, ref in enumerate(refs):
        for b in range(4):
            for s in range(8):
                rows, lanes = slice(8 * b, 8 * b + 8), slice(128 * s, 128 * s + 128)
                tile = ref[rows, lanes] if len(ref.shape) == 2 else ref[which, rows, lanes]
                out[pl.ds(8 * (32 * place + 8 * b) + s, 8, stride=8), :] = tile


def pack_waves(core_ref, now, before, velocity, cotangent, mine, given):
    core = core_ref[0]
    for which, out in ((core, mine), (1 - core, given)):
        pack_rows(which, (now, before, velocity), out)
        out[8 * 96 : 8 * 100, :] = cotangent[...]


def pack_adjoints(core_ref, last, after, mine, given):
    core = core_ref[0]
    for which, out in ((core, mine), (1 - core, given)):
        pack_rows(which, (last, after), out)


def receiver_kernel(
    core_ref, chip_ref, source_col, rec_first, rec_last, rec_count, observed, source, counts, recorded
):
    core = core_ref[0]
    lit = jnp.where(chip_ref[0] == 0, 1.0, 0.0)
    lane = lax.broadcasted_iota(jnp.int32, (8, 128), 1)
    column = lax.broadcasted_iota(jnp.int32, (8, 128), 0) * 128 + lane
    source[...] = jnp.where(column == source_col[core], lit, 0.0)
    slot = lax.broadcasted_iota(jnp.int32, (128, 128), 0)
    live = slot < rec_count[core]
    span = (rec_last[core] - rec_first[core]).astype(jnp.float32)
    gaps = jnp.full((128, 128), (rec_count[core] - 1).astype(jnp.float32))
    way = slot.astype(jnp.float32) * span
    steps = jnp.floor(way / gaps)
    rest = way - steps * gaps
    steps = jnp.where(rest < 0.0, steps - 1.0, jnp.where(rest >= gaps, steps + 1.0, steps))
    placed = rec_first[core] + steps.astype(jnp.int32)
    values = observed[core]
    high, rest = split(values)
    rest = values - high.astype(jnp.float32)
    middle, low = split(rest)
    terms = jnp.concatenate([high, middle, low, jnp.ones((16, 128), jnp.bfloat16)], axis=0)
    wide = lax.broadcasted_iota(jnp.int32, (128, 128), 1)
    for s in range(8):
        table = jnp.where(live & (placed == wide + 128 * s), lit, 0.0).astype(jnp.bfloat16)
        result = mul(terms, table)
        counts[s : s + 1, :] = result[48:49]
        recorded[pl.ds(s, 16, stride=8), :] = (result[0:16] + result[16:32]) + result[32:48]


def split(x):
    high = x.astype(jnp.bfloat16)
    low = (x - high.astype(jnp.float32)).astype(jnp.bfloat16)
    return high, low


def window(ref, rows, first, count, shift):
    start = SIDE + first + shift
    base = start // 128 * 128
    offset = start - base
    if offset == 0:
        return ref[rows, base : base + count]
    wide = ref[rows, base : base + count + 128]
    return pltpu.roll(wide, count + 128 - offset, 1)[:, :count]


def mul(left, right):
    return jnp.dot(left, right, preferred_element_type=jnp.float32)


def mul_t(left, right):
    return lax.dot_general(
        left, right, (((1,), (1,)), ((), ())), preferred_element_type=jnp.float32
    )


def network_kernel(
    core, row_base, col_base, summed, arrived, velocity_wide, cotangent_rows, first_w, middle_w, back_w, last_w,
    new_velocity, grads,
    base, taps, packed, slope_one_d, before, products, last_products, pairs, hidden_one, slope_own, packed_two, packed_slope, own_terms, updates, inside, own,
):
    lane = lax.broadcasted_iota(jnp.int32, (8, 128), 1)
    sub = lax.broadcasted_iota(jnp.int32, (8, 128), 0)
    lower = core[0] == 0
    edges = summed[40:48, :]
    other_edges = arrived[8:16, :]
    edge_rows = jnp.where(
        lower,
        jnp.where(lane < 3, pltpu.roll(other_edges, 67, 1), pltpu.roll(edges, 3, 1)),
        jnp.where(
            (lane >= 35) & (lane < 38), pltpu.roll(other_edges, 35, 1), pltpu.roll(edges, 99, 1)
        ),
    )
    turned = jnp.transpose(
        jnp.concatenate(
            [edge_rows, pltpu.roll(edges, 65, 1), jnp.zeros((112, 128), jnp.float32)], axis=0
        )
    )[0:40]
    main = summed[0:40, :]
    tile = pltpu.roll(arrived[0:8, :], 3, 0)
    down = pltpu.roll(main, 3, 0)
    up = pltpu.roll(main, 35, 0)
    low_case = jnp.concatenate([jnp.where(sub < 3, tile, down[0:8]), down[8:40]], axis=0)
    high_case = jnp.concatenate(
        [up[0:32], jnp.where((sub >= 3) & (sub < 6), tile, up[32:40])], axis=0
    )
    image = jnp.where(lower, low_case, high_case)
    lanes = lax.broadcasted_iota(jnp.int32, (40, 128), 1)
    scale = 1.0 / float(STEPS * 16) ** 0.5
    shifted = pltpu.roll(image, 3, 1)
    image_a = jnp.where(lanes < 3, turned, shifted) * scale
    image_b = jnp.where(lanes < 3, shifted, jnp.where(lanes < 6, turned, 0.0)) * scale
    shifted = pltpu.roll(cotangent_rows[...], 3, 1)
    sides = pltpu.roll(turned, 121, 1)
    cot_a = jnp.where(lanes < 1, 0.0, jnp.where(lanes < 3, sides, shifted))
    cot_b = jnp.where(lanes < 3, shifted, jnp.where(lanes < 5, sides, 0.0))
    velocity_all = velocity_wide[...]

    base[...] = jnp.zeros(base.shape, jnp.float32)
    wide_rows = [
        velocity_all,
        jnp.concatenate([image_a, image_b], axis=1),
        jnp.concatenate([cot_a, cot_b], axis=1),
    ]
    for channel, wide in enumerate(wide_rows):
        pieces = {}
        for r in range(38):
            start = LINE * r
            v, offset = start // 128, start % 128
            row = wide[r : r + 1, :]
            if offset:
                row = pltpu.roll(row, offset, 1)
            pieces.setdefault(v, []).append(row[:, 0:128])
            pieces.setdefault(v + 1, []).append(row[:, 128:256])
        for v, found in pieces.items():
            total = found[0]
            for piece in found[1:]:
                total = total + piece
            base[channel : channel + 1, SIDE + 128 * v : SIDE + 128 * v + 128] = total

    parts = [(p * PART, slice(p * PART, (p + 1) * PART)) for p in range(FLAT // PART)]
    for first, cut in parts:
        at = (lax.broadcasted_iota(jnp.int32, (8, PART), 1) + first).astype(jnp.float32)
        row_of = jnp.floor((at + 0.5) * (1.0 / LINE)).astype(jnp.int32)
        col_of = lax.broadcasted_iota(jnp.int32, (8, PART), 1) + first - LINE * row_of
        grid_row, grid_col = row_of + row_base[0], col_of + col_base[0]
        mask = (row_of < 38) & (col_of < 134)
        mask = mask & (grid_row >= 0) & (grid_row < 1024) & (grid_col >= 0) & (grid_col < 1024)
        inside[:, cut] = jnp.where(mask, 1.0, 0.0)
        mask = (row_of >= 3) & (row_of < 35) & (col_of >= 3) & (col_of < 131)
        own[:, cut] = jnp.where(mask, 1.0, 0.0)
    all_rows = slice(0, 8)
    padding = jnp.zeros((8, PART), jnp.float32)
    for first, cut in parts:
        gathered = [window(base, all_rows, first, PART, shift) for shift in TAPS]
        high, low = split(jnp.concatenate(gathered + [padding], axis=0))
        taps[0:80, cut] = high
        taps[80:160, cut] = low
        result = mul(first_w[...], taps[:, cut])
        result = result[0:64] + result[64:128]
        value = result[0:CH]
        pulled = jax.nn.sigmoid(value)
        slope_one_d[:, cut] = pulled * (1.0 + value * (1.0 - pulled))
        mask = inside[:, cut] > 0.0
        mask = jnp.concatenate([mask] * 4, axis=0)
        hidden = jnp.where(mask, value * pulled, 0.0)
        hidden_one[:, SIDE + first : SIDE + first + PART] = hidden
        before[:, cut] = result[CH : 2 * CH]
        high, low = split(hidden)
        packed[0:32, cut] = high
        packed[32:64, cut] = low
        packed[64:96, cut] = high
    edge = jnp.zeros((CH, SIDE), jnp.float32)
    hidden_one[:, 0:SIDE] = edge
    hidden_one[:, SIDE + FLAT :] = edge
    zero_edge = jnp.zeros((9 * CH, SIDE), jnp.float32)
    products[:, 0:SIDE] = zero_edge
    products[:, SIDE + FLAT :] = zero_edge
    last_products[:, 0:SIDE] = jnp.zeros((16, SIDE), jnp.float32)
    last_products[:, SIDE + FLAT :] = jnp.zeros((16, SIDE), jnp.float32)

    for first, cut in parts:
        products[:, SIDE + first : SIDE + first + PART] = mul(middle_w[...], packed[:, cut])
    for first, cut in parts:
        mask = inside[:, cut] > 0.0
        here = own[:, cut] > 0.0
        for g in range(4):
            total = None
            for tap, shift in enumerate(TAPS):
                piece = window(
                    products, slice(tap * CH + 8 * g, tap * CH + 8 * g + 8), first, PART, shift
                )
                total = piece if total is None else total + piece
            pulled = jax.nn.sigmoid(total)
            rows = slice(8 * g, 8 * g + 8)
            hidden = jnp.where(mask, total * pulled, 0.0)
            slope = jnp.where(
                mask, before[rows, cut] * (pulled * (1.0 + total * (1.0 - pulled))), 0.0
            )
            pairs[rows, cut] = hidden
            slope_own[rows, cut] = slope
        hidden = pairs[:, cut]
        slope = slope_own[:, cut]
        high, low = split(hidden)
        packed_two[0:32, cut] = high
        packed_two[32:64, cut] = low
        packed_two[64:96, cut] = high
        here = jnp.concatenate([here] * 4, axis=0)
        high, low = split(jnp.where(here, hidden, 0.0))
        own_terms[32:64, cut] = high
        own_terms[96:128, cut] = low
        high, low = split(slope)
        packed_slope[0:32, cut] = high
        packed_slope[32:64, cut] = low
        packed_slope[64:96, cut] = high
        last_products[:, SIDE + first : SIDE + first + PART] = mul(last_w[...], packed_two[:, cut])

    wide_sub = lax.broadcasted_iota(jnp.int32, (8, PART), 0)
    for first, cut in parts:
        total = jnp.zeros((8, PART), jnp.float32)
        for tap, shift in enumerate(TAPS):
            rows = slice(0, 8) if tap < 8 else slice(8, 16)
            piece = window(last_products, rows, first, PART, shift)
            total = total + jnp.where(wide_sub == tap % 8, piece, 0.0)
        updates[0:1, cut] = jnp.sum(total, axis=0, keepdims=True)
    velocity_here = pltpu.roll(velocity_all, 253, 1)[:, 0:128]
    for r in range(32):
        start = LINE * (r + 3) + 3
        v, offset = start // 128, start % 128
        row = updates[0:1, 128 * v : 128 * v + 256]
        if offset:
            row = pltpu.roll(row, 256 - offset, 1)
        new_velocity[r : r + 1, :] = velocity_here[r + 3 : r + 4] + row[:, 0:128]

    for first, cut in parts:
        products[:, SIDE + first : SIDE + first + PART] = mul(back_w[...], packed_slope[:, cut])
    for first, cut in parts:
        here = own[:, cut] > 0.0
        for g in range(4):
            total = None
            for tap, shift in enumerate(TAPS):
                piece = window(
                    products, slice(tap * CH + 8 * g, tap * CH + 8 * g + 8), first, PART, -shift
                )
                total = piece if total is None else total + piece
            rows = slice(8 * g, 8 * g + 8)
            pairs[rows, cut] = jnp.where(here, total * slope_one_d[rows, cut], 0.0)
        high, low = split(pairs[:, cut])
        own_terms[0:32, cut] = high
        own_terms[64:96, cut] = low

    middle_sum = jnp.zeros((CH, 9 * CH), jnp.float32)
    outer_sum = jnp.zeros((64, 80), jnp.float32)
    for first, cut in parts:
        here = jnp.concatenate([own[:, cut] > 0.0] * 4, axis=0)
        shifted = jnp.concatenate(
            [window(hidden_one, slice(0, CH), first, PART, shift) for shift in TAPS], axis=0
        )
        high, low = split(shifted)
        slope_high, slope_low = split(jnp.where(here, slope_own[:, cut], 0.0))
        both = mul_t(jnp.concatenate([slope_high, slope_low], axis=0), high)
        middle_sum = middle_sum + (both[0:CH] + both[CH:] + mul_t(slope_high, low))
        terms = own_terms[:, cut]
        both = mul_t(terms, taps[0:80, cut])
        outer_sum = outer_sum + (both[0:64] + both[64:128] + mul_t(terms[0:64], taps[80:160, cut]))
    blank = jnp.zeros((CH, 48), jnp.float32)
    first_sum = jnp.concatenate([outer_sum[0:CH], blank], axis=1)
    last_sum = jnp.concatenate([outer_sum[CH:64], blank], axis=1)
    lanes = lax.broadcasted_iota(jnp.int32, (CH, 128), 1)
    tail = jnp.concatenate([middle_sum[:, 256:288], jnp.zeros((CH, 96), jnp.float32)], axis=1)
    for tap in range(9):
        moved = pltpu.roll(first_sum, (32 + 2 * tap - 8 * tap) % 128, 1)
        tail = jnp.where((lanes >= 32 + 2 * tap) & (lanes < 34 + 2 * tap), moved, tail)
    grads[0:CH, 0:256] = middle_sum[:, 0:256]
    grads[0:CH, 256:384] = tail
    columns = jnp.transpose(jnp.concatenate([last_sum, jnp.zeros((96, 128), jnp.float32)], axis=0))
    line = lax.broadcasted_iota(jnp.int32, (1, 128), 1) // 32
    for part in range(3):
        row = jnp.zeros((1, 128), jnp.float32)
        for q in range(4):
            tap = 4 * part + q
            if tap < 9:
                at = 8 * (8 - tap) + 2
                row = jnp.where(line == q, pltpu.roll(columns[at : at + 1], 32 * q, 1), row)
        grads[CH : CH + 1, 128 * part : 128 * part + 128] = row
    grads[CH + 1 : CH + 8, :] = jnp.zeros((7, 384), jnp.float32)


def last_kernel(one, other, grad_in, grad_mid, grad_out):
    total = one[...] + other[...]
    grad_mid[...] = total[0:CH, 0:288]
    grad_in[...] = jnp.transpose(total[0:CH, 256:384])[32:50]
    grad_out[...] = total[CH : CH + 1, 0:288]


def vmem():
    return pl.BlockSpec(memory_space=pltpu.VMEM)


def anywhere():
    return pl.BlockSpec(memory_space=pl.ANY)


def in_hbm():
    return pl.BlockSpec(memory_space=pltpu.HBM)


def smem():
    return pl.BlockSpec(memory_space=pltpu.SMEM)


def f32(*shape):
    return jax.ShapeDtypeStruct(shape, jnp.float32)


def scratch(*shape, dtype=jnp.float32):
    return pltpu.VMEM(shape, dtype)


def call(kernel, in_specs, out_shape, scratch_shapes, *operands, out_specs=None):
    many = isinstance(out_shape, tuple)
    default = tuple(vmem() for _ in out_shape) if many else vmem()
    return pl.pallas_call(
        kernel,
        in_specs=in_specs,
        out_specs=default if out_specs is None else out_specs,
        out_shape=out_shape,
        scratch_shapes=scratch_shapes,
        compiler_params=pltpu.CompilerParams(vmem_limit_bytes=vmem_limit),
    )(*operands)


def stacked_weights(weights):
    high = weights.astype(jnp.bfloat16)
    low = (weights - lax.reduce_precision(weights, 8, 7)).astype(jnp.bfloat16)
    return high, low


def three_terms(weights):
    high, low = stacked_weights(weights)
    return jnp.concatenate([high, high, low], axis=1)


def over_pairs(x, axis, groups):
    return x + lax.ppermute(x, axis, [(a, b) for a, b in groups] + [(b, a) for a, b in groups])


def over_fours(x, axis, groups):
    near, far, cross = (
        lax.ppermute(x, axis, [(group[i], group[i ^ turn]) for group in groups for i in range(4)])
        for turn in (1, 2, 3)
    )
    return (x + near) + (far + cross)


def on_device(
    velocity,
    wave_now,
    wave_before,
    adjoint_last,
    adjoint_after,
    wavelet,
    source_col,
    rec_first,
    rec_last,
    rec_count,
    observed,
    conv_in,
    conv_mid,
    conv_out,
    cotangent,
):
    core = lax.axis_index(CORE)
    chip = lax.axis_index(CHIPS)
    cell = lax.axis_index(CELL)
    chips = lax.axis_size(CHIPS)
    core_id, chip_id, cell_id = (x.reshape(1).astype(jnp.int32) for x in (core, chip, cell))
    mine, given = call(
        pack_waves,
        [smem()] + [vmem()] * 4,
        (f32(WAVES * 8, 128), f32(WAVES * 8, 128)),
        [],
        core_id,
        wave_now,
        wave_before,
        velocity,
        cotangent,
    )
    swap = [(0, 1), (1, 0)]
    up = [(i, i + 1) for i in range(chips - 1)]
    down = [(i + 1, i) for i in range(chips - 1)]
    theirs = lax.ppermute(given, CORE, swap)
    waves = jnp.concatenate([mine, theirs]).reshape(2 * WAVES, 8, 128)
    low = lax.ppermute(waves, CHIPS, up)
    high = lax.ppermute(waves, CHIPS, down)
    (
        waves_kept, adjoint_last, adjoint_after, source_col, rec_first, rec_last, rec_count, observed,
    ) = lax.optimization_barrier(
        (waves, adjoint_last, adjoint_after, source_col, rec_first, rec_last, rec_count, observed)
    )
    mine, given = call(
        pack_adjoints,
        [smem()] + [vmem()] * 2,
        (f32(CHIP * 8, 128), f32(CHIP * 8, 128)),
        [],
        core_id,
        adjoint_last,
        adjoint_after,
    )
    theirs = lax.ppermute(given, CORE, swap)
    adjoints = jnp.concatenate([mine, theirs]).reshape(2 * CHIP, 8, 128)
    source, counts, recorded = call(
        receiver_kernel,
        [smem()] * 6 + [vmem()],
        (f32(8, 128), f32(8, 128), f32(STEPS * 8, 128)),
        [],
        core_id,
        chip_id,
        source_col,
        rec_first,
        rec_last,
        rec_count,
        observed,
    )
    adjoints, counts, recorded, source = lax.optimization_barrier(
        (adjoints, counts, recorded, source)
    )
    low_adjoint = lax.ppermute(adjoints, CHIPS, up)
    high_adjoint = lax.ppermute(adjoints, CHIPS, down)

    stored, speeds, velocity_rows, cot_rows = call(
        forward_kernel,
        [smem()] * 2 + [vmem(), in_hbm(), anywhere(), in_hbm()],
        (f32(STEPS, CHIP, 8, 128), f32(WIDE, 8, 128), f32(40, 8, 128), f32(40, 128)),
        [
            scratch(2, WIDE, 8, 128),
            scratch(WIDE, 8, 128),
            scratch(10, 8, 128),
            pltpu.SemaphoreType.DMA((18,)),
            pltpu.SemaphoreType.DMA((4,)),
            pltpu.SemaphoreType.DMA((2,)),
        ],
        core_id,
        wavelet,
        source,
        low,
        waves_kept,
        high,
        out_specs=(in_hbm(), vmem(), vmem(), vmem()),
    )
    pieces = call(
        adjoint_kernel,
        [smem()] * 2 + [vmem()] * 2 + [in_hbm(), anywhere(), in_hbm(), vmem(), in_hbm(), vmem()],
        f32(16, 48, 128),
        [
            scratch(2, WIDE, 8, 128),
            scratch(CHIP, 8, 128),
            scratch(8, 128, 128),
            scratch(2, CHIP, 8, 128),
            pltpu.SemaphoreType.DMA((12,)),
            pltpu.SemaphoreType.DMA((2,)),
        ],
        core_id,
        cell_id,
        counts,
        recorded.reshape(STEPS, 8, 128),
        low_adjoint,
        adjoints,
        high_adjoint,
        speeds,
        stored,
        cot_rows,
    )
    pieces, velocity_rows, conv_in, conv_mid, conv_out = lax.optimization_barrier(
        (pieces, velocity_rows, conv_in, conv_mid, conv_out)
    )
    lower = core == 0
    velocity_wide = lax.dynamic_slice_in_dim(
        jnp.pad(velocity_rows.reshape(40, 1024), ((0, 0), (3, 253))), 128 * cell, 256, 1
    )
    velocity_wide = jnp.where(jnp.arange(256)[None, :] < 134, velocity_wide, 0.0)
    first = jnp.pad(conv_in.reshape(CH, 9, 2), ((0, 0), (0, 1), (0, 6))).reshape(CH, 80)
    pulling = jnp.pad(
        conv_out.reshape(9, CH)[::-1].T[:, :, None], ((0, 0), (0, 1), (2, 5))
    ).reshape(CH, 80)
    first_high, first_low = stacked_weights(jnp.concatenate([first, pulling]))
    first_w = jnp.concatenate(
        [
            jnp.concatenate([first_high, first_high], axis=1),
            jnp.concatenate([first_low, jnp.zeros_like(first_low)], axis=1),
        ]
    )
    middle = conv_mid.reshape(CH, 9, CH)
    middle_w = three_terms(middle.transpose(1, 0, 2).reshape(9 * CH, CH))
    back_w = three_terms(middle.transpose(1, 2, 0).reshape(9 * CH, CH))
    last_w = three_terms(jnp.pad(conv_out.reshape(9, CH), ((0, 7), (0, 0))))

    summed = jnp.sum(lax.all_to_all(pieces, SUMMED, 0, 0, tiled=True), axis=0)
    edge_rows = jnp.concatenate([jnp.where(lower, summed[0:8], summed[32:40]), summed[40:48]])
    bands = lax.axis_size(BAND)
    outward = [(b, b - 1) for b in range(2, bands, 2)] + [(b, b + 1) for b in range(1, bands - 1, 2)]
    arrived = lax.ppermute(edge_rows, BAND, outward)

    bf16 = jnp.bfloat16
    new_velocity, grads = call(
        network_kernel,
        [smem()] * 3 + [vmem()] * 8,
        (f32(32, 128), f32(CH + 8, 384)),
        [
            scratch(8, FLAT + 2 * SIDE),
            scratch(160, FLAT, dtype=bf16),
            scratch(96, FLAT, dtype=bf16),
            scratch(CH, FLAT),
            scratch(CH, FLAT),
            scratch(9 * CH, FLAT + 2 * SIDE),
            scratch(16, FLAT + 2 * SIDE),
            scratch(CH, FLAT),
            scratch(CH, FLAT + 2 * SIDE),
            scratch(CH, FLAT),
            scratch(96, FLAT, dtype=bf16),
            scratch(96, FLAT, dtype=bf16),
            scratch(128, FLAT, dtype=bf16),
            scratch(8, FLAT),
            scratch(8, FLAT),
            scratch(8, FLAT),
        ],
        core_id,
        (64 * chip + 32 * core - 3).reshape(1).astype(jnp.int32),
        (128 * cell - 3).reshape(1).astype(jnp.int32),
        summed,
        arrived,
        velocity_wide,
        cot_rows,
        first_w,
        middle_w,
        back_w,
        last_w,
    )
    total = over_pairs(grads, CORE, [(0, 1)])
    total = over_fours(total, "shot", [(0, 1, 2, 3)])
    total = over_fours(total, ("band_0", "net"), [(0, 1, 2, 3)])
    total = over_fours(total, "band_1", [(0, 1, 2, 3), (4, 5, 6, 7)])
    other = lax.ppermute(total, "band_1", [(i, 7 - i) for i in range(8)])
    grad_in, grad_mid, grad_out = call(
        last_kernel,
        [vmem()] * 2,
        (f32(18, CH), f32(CH, 9 * CH), f32(1, 9 * CH)),
        [],
        total,
        other,
    )
    return new_velocity, grad_in.T, grad_mid, grad_out


def solution(mesh):
    split_mesh = Mesh(
        mesh.devices.reshape(mesh.shape["shot"], 2, 8, 2, mesh.shape["net"]),
        ("shot", "band_0", "band_1", "band_2", "net"),
    )
    placed = (
        P(BAND, None),
        P(CELL, BAND, None),
        P(CELL, BAND, None),
        P(CELL, BAND, None),
        P(CELL, BAND, None),
        P(CELL, None),
        P(CELL),
        P(CELL),
        P(CELL),
        P(CELL),
        P(CELL, None, None),
        P(),
        P(),
        P(),
        P(BAND, CELL),
    )
    return jax.shard_map(
        on_device,
        mesh=split_mesh,
        in_specs=placed,
        out_specs=(P(BAND, CELL), P(), P(), P()),
        check_vma=False,
    )
```

```python
import jax
import jax.numpy as jnp
from jax import lax
from jax.experimental import pallas as pl
from jax.experimental.pallas import tpu as pltpu
from jax.sharding import Mesh
from jax.sharding import PartitionSpec as P

BAND = ("band_0", "band_1", "band_2")
CHIPS = ("band_0", "band_1")
CORE = "band_2"
CELL = ("shot", "net")
SUMMED = ("shot", "band_2", "net")

coefficients = (-205.0 / 72.0, 8.0 / 5.0, -1.0 / 5.0, 8.0 / 315.0, -1.0 / 560.0)
speed_factor = 0.11
source_depth = 2
receiver_depth = 3
highest = lax.Precision.HIGHEST

STEPS = 16
CHIP = 64
BLOCK = 64
WAVES = 100
WIDE = 3 * CHIP
LINE = 136
FLAT = 42 * 128
PART = 768
SIDE = 256
CH = 32
vmem_limit = 56 * 1024 * 1024
TAPS = [(down - 1) * LINE + (across - 1) for down in range(3) for across in range(3)]


def stencil_constants():
    lane = lax.broadcasted_iota(jnp.int32, (8, 128), 1)
    column = lax.broadcasted_iota(jnp.int32, (8, 128), 0) * 128 + lane
    c0, c1, c2, c3, c4 = coefficients

    def where(mask, value):
        return jnp.where(mask, jnp.float32(value), jnp.float32(0.0))

    return dict(
        low1=lane < 1,
        low3=lane < 3,
        high1=lane >= 127,
        high3=lane >= 125,
        c1u=where(column != 0, c1),
        c1v=where(column != 1023, c1),
        c2p=where((column != 1021) & (column != 1022), c2),
        c3p=where(column <= 1020, c3),
        c4p=where((column <= 1020) & (column != 0), c4),
        c2m=where((column != 1) & (column != 2), c2),
        c3m=where(column >= 3, c3),
        c4m=where((column >= 3) & (column != 1023), c4),
    )


def from_left(x, count, mask):
    turned = pltpu.roll(x, count, 1)
    return jnp.where(mask, pltpu.roll(turned, 1, 0), turned)


def from_right(x, count, mask):
    turned = pltpu.roll(x, 128 - count, 1)
    return jnp.where(mask, pltpu.roll(turned, 7, 0), turned)


def advance(k, fields, speeds, now, step):
    other = 1 - now
    c0, c1, c2, c3, c4 = coefficients

    def block(first, count):
        rows = [fields[now, first - 4 + i] for i in range(count + 8)]
        prior = [fields[other, first + i] for i in range(count)]
        speed = [speeds[first + i] for i in range(count)]
        middle = rows[4 : 4 + count]
        left = [from_left(x, 1, k["low1"]) for x in middle]
        right = [from_right(x, 1, k["high1"]) for x in middle]
        ahead = [
            k["c2p"] * right[i] + k["c3p"] * middle[i] + k["c4p"] * left[i] for i in range(count)
        ]
        behind = [
            k["c2m"] * left[i] + k["c3m"] * middle[i] + k["c4m"] * right[i] for i in range(count)
        ]
        ahead = [from_left(x, 3, k["low3"]) for x in ahead]
        behind = [from_right(x, 3, k["high3"]) for x in behind]
        fresh = []
        for i in range(count):
            total = k["c1u"] * left[i] + k["c1v"] * right[i] + (2.0 * c0) * middle[i]
            for reach, weight in ((1, c1), (2, c2), (3, c3), (4, c4)):
                total = total + weight * (rows[i + 4 - reach] + rows[i + 4 + reach])
            total = total + (ahead[i] + behind[i])
            fresh.append((middle[i] + middle[i]) - prior[i] + speed[i] * total)
        for i in range(count):
            fields[other, first + i] = fresh[i]

    first, count = 4 * step, WIDE - 8 * step
    whole = count // BLOCK

    def body(i, carry):
        block(first + BLOCK * i, BLOCK)
        return carry

    lax.fori_loop(0, whole, body, 0)
    if count % BLOCK:
        block(first + BLOCK * whole, count % BLOCK)


def band_copies(core, packs, stride, targets, sems):
    copies = []
    for place, pack in zip((0, CHIP, 2 * CHIP), packs):
        for part in range(2):
            band = core if part == 0 else 1 - core
            for i, target in enumerate(targets):
                copies.append(
                    pltpu.make_async_copy(
                        pack.at[pl.ds(stride * part + 32 * i, 32)],
                        target.at[pl.ds(place + 32 * band, 32)],
                        sems.at[len(copies)],
                    )
                )
    return copies


def forward_kernel(
    core_ref, pulses, source, low, mid, high,
    stored, speeds, velocity_rows, cot_rows,
    fields, velocity, cot, sems, cot_sems, out_sems,
):
    core = core_ref[0]
    copies = band_copies(core, (low, mid, high), WAVES, (fields.at[0], fields.at[1], velocity), sems)
    cot_copies = [
        pltpu.make_async_copy(low.at[WAVES * (1 - core) + 99], cot.at[0], cot_sems.at[0]),
        pltpu.make_async_copy(
            mid.at[pl.ds(96, 4)], cot.at[pl.ds(1 + 4 * core, 4)], cot_sems.at[1]
        ),
        pltpu.make_async_copy(
            mid.at[pl.ds(WAVES + 96, 4)], cot.at[pl.ds(5 - 4 * core, 4)], cot_sems.at[2]
        ),
        pltpu.make_async_copy(high.at[WAVES * core + 96], cot.at[9], cot_sems.at[3]),
    ]
    for copy in copies + cot_copies:
        copy.start()
    for copy in copies + cot_copies:
        copy.wait()

    def square(i, carry):
        at = pl.ds(8 * i, 8)
        scaled = velocity[at] * speed_factor
        speeds[at] = scaled * scaled
        return carry

    lax.fori_loop(0, WIDE // 8, square, 0)
    for i in range(5):
        velocity_rows[8 * i : 8 * i + 8] = velocity[pl.ds(CHIP - 3 + 32 * core + 8 * i, 8)]
    tiles = cot[pl.ds(4 * core, 6)].reshape(48, 128)
    cot_rows[...] = pltpu.roll(tiles, 43, 0)[0:40]
    k = stencil_constants()
    saves = []
    for n in range(STEPS):
        now = n % 2
        if n >= 2:
            saves[n - 2].wait()
        advance(k, fields, speeds, now, n + 1)
        row = CHIP + source_depth
        fields[1 - now, row] = fields[1 - now, row] + pulses[core, n] * source[...]
        saves.append(
            pltpu.make_async_copy(
                fields.at[1 - now, pl.ds(CHIP, CHIP)], stored.at[n], out_sems.at[n % 2]
            )
        )
        saves[n].start()
    saves[STEPS - 2].wait()
    saves[STEPS - 1].wait()


def adjoint_kernel(
    core_ref, cell_ref, counts, recorded, low, mid, high, speeds, stored, cot_rows,
    out,
    fields, image3, turned, passed, sems, in_sems,
):
    core = core_ref[0]
    cell = cell_ref[0]
    copies = band_copies(core, (low, mid, high), CHIP, (fields.at[0], fields.at[1]), sems)
    loads = [
        pltpu.make_async_copy(stored.at[n], passed.at[n % 2], in_sems.at[n % 2])
        for n in range(STEPS)
    ]
    loads[STEPS - 1].start()
    for copy in copies:
        copy.start()
    for copy in copies:
        copy.wait()
    k = stencil_constants()
    for m in range(STEPS):
        now = m % 2
        n = STEPS - 1 - m
        loads[n].wait()
        if n:
            loads[n - 1].start()
        advance(k, fields, speeds, now, m + 1)
        row = CHIP + receiver_depth
        push = counts[...] * passed[n % 2, receiver_depth] - recorded[n]
        fields[1 - now, row] = fields[1 - now, row] + push

        for at in range(0, CHIP, 8):
            product = passed[n % 2, at : at + 8] * fields[1 - now, CHIP + at : CHIP + at + 8]
            if m:
                product = image3[at : at + 8] + product
            image3[at : at + 8] = product
    image = image3.reshape(CHIP * 8, 128)
    blank = jnp.zeros((64, 128), jnp.float32)
    for j in range(8):
        block = jnp.concatenate(
            [image[pl.ds(64 * b + j, 8, stride=8), :] for b in range(8)], axis=0
        )
        for half in range(2):
            d = ((j // 2) * 2 + half) * 2 + j % 2
            out[d, 0:40, :] = block[24 * half : 24 * half + 40]
        turned[j] = jnp.transpose(jnp.concatenate([block, blank], axis=0))
    sub = lax.broadcasted_iota(jnp.int32, (8, 128), 0)
    lane = lax.broadcasted_iota(jnp.int32, (8, 128), 1)
    columns = jnp.transpose(
        jnp.concatenate([cot_rows[...], jnp.zeros((88, 128), jnp.float32)], axis=0)
    )
    here = (lane >= 64) & (lane < 100)
    to_right = pltpu.roll(pltpu.roll(columns[120:128], 2, 0), 63, 1)
    to_right = jnp.where(here & (sub < 2), to_right, 0.0)
    to_left = pltpu.roll(pltpu.roll(columns[0:8], 2, 0), 63, 1)
    to_left = jnp.where(here & (sub >= 2) & (sub < 4), to_left, 0.0)
    for j in range(8):
        edges = jnp.zeros((8, 128), jnp.float32)
        if j > 0:
            edges = jnp.where(sub < 3, pltpu.roll(turned[j - 1, 120:128, :], 3, 0), edges)
        if j < 7:
            edges = jnp.where(
                (sub >= 3) & (sub < 6), pltpu.roll(turned[j + 1, 0:8, :], 3, 0), edges
            )
        for half in range(2):
            d = ((j // 2) * 2 + half) * 2 + j % 2
            extra = jnp.where((cell == j - 1) & (core == half), to_right, 0.0)
            extra = jnp.where((cell == j + 1) & (core == half), to_left, extra)
            out[d, 40:48, :] = edges + extra


def pack_rows(which, refs, out):
    for place, ref in enumerate(refs):
        for b in range(4):
            for s in range(8):
                rows, lanes = slice(8 * b, 8 * b + 8), slice(128 * s, 128 * s + 128)
                tile = ref[rows, lanes] if len(ref.shape) == 2 else ref[which, rows, lanes]
                out[pl.ds(8 * (32 * place + 8 * b) + s, 8, stride=8), :] = tile


def pack_kernel(
    core_ref, now, before, last, after, velocity, cotangent, mine_w, given_w, mine_a, given_a
):
    core = core_ref[0]
    for which, waves, adjoints in ((core, mine_w, mine_a), (1 - core, given_w, given_a)):
        pack_rows(which, (now, before, velocity), waves)
        waves[8 * 96 : 8 * 100, :] = cotangent[...]
        pack_rows(which, (last, after), adjoints)


def receiver_kernel(
    core_ref, chip_ref, source_col, rec_first, rec_last, rec_count, observed, source, counts, recorded
):
    core = core_ref[0]
    lit = jnp.where(chip_ref[0] == 0, 1.0, 0.0)
    lane = lax.broadcasted_iota(jnp.int32, (8, 128), 1)
    column = lax.broadcasted_iota(jnp.int32, (8, 128), 0) * 128 + lane
    source[...] = jnp.where(column == source_col[core], lit, 0.0)
    slot = lax.broadcasted_iota(jnp.int32, (128, 128), 0)
    live = slot < rec_count[core]
    span = (rec_last[core] - rec_first[core]).astype(jnp.float32)
    gaps = jnp.full((128, 128), (rec_count[core] - 1).astype(jnp.float32))
    way = slot.astype(jnp.float32) * span
    steps = jnp.floor(way / gaps)
    rest = way - steps * gaps
    steps = jnp.where(rest < 0.0, steps - 1.0, jnp.where(rest >= gaps, steps + 1.0, steps))
    placed = rec_first[core] + steps.astype(jnp.int32)
    values = observed[core]
    high, rest = split(values)
    rest = values - high.astype(jnp.float32)
    middle, low = split(rest)
    terms = jnp.concatenate([high, middle, low, jnp.ones((16, 128), jnp.bfloat16)], axis=0)
    wide = lax.broadcasted_iota(jnp.int32, (128, 128), 1)
    for s in range(8):
        table = jnp.where(live & (placed == wide + 128 * s), lit, 0.0).astype(jnp.bfloat16)
        result = mul(terms, table)
        counts[s : s + 1, :] = result[48:49]
        recorded[pl.ds(s, 16, stride=8), :] = (result[0:16] + result[16:32]) + result[32:48]


def split(x):
    high = x.astype(jnp.bfloat16)
    low = (x - high.astype(jnp.float32)).astype(jnp.bfloat16)
    return high, low


def window(ref, rows, first, count, shift):
    start = SIDE + first + shift
    base = start // 128 * 128
    offset = start - base
    if offset == 0:
        return ref[rows, base : base + count]
    wide = ref[rows, base : base + count + 128]
    return pltpu.roll(wide, count + 128 - offset, 1)[:, :count]


def mul(left, right):
    return jnp.dot(left, right, preferred_element_type=jnp.float32)


def mul_t(left, right):
    return lax.dot_general(
        left, right, (((1,), (1,)), ((), ())), preferred_element_type=jnp.float32
    )


def network_kernel(
    core, row_base, col_base, summed, arrived, velocity_wide, cotangent_rows, first_w, middle_w, back_w, last_w,
    new_velocity, grads,
    base, taps, packed, slope_one_d, before, products, last_products, pairs, hidden_one, slope_own, packed_two, packed_slope, own_terms, updates, inside, own,
):
    lane = lax.broadcasted_iota(jnp.int32, (8, 128), 1)
    sub = lax.broadcasted_iota(jnp.int32, (8, 128), 0)
    lower = core[0] == 0
    edges = summed[40:48, :]
    other_edges = arrived[8:16, :]
    edge_rows = jnp.where(
        lower,
        jnp.where(lane < 3, pltpu.roll(other_edges, 67, 1), pltpu.roll(edges, 3, 1)),
        jnp.where(
            (lane >= 35) & (lane < 38), pltpu.roll(other_edges, 35, 1), pltpu.roll(edges, 99, 1)
        ),
    )
    turned = jnp.transpose(
        jnp.concatenate(
            [edge_rows, pltpu.roll(edges, 65, 1), jnp.zeros((112, 128), jnp.float32)], axis=0
        )
    )[0:40]
    main = summed[0:40, :]
    tile = pltpu.roll(arrived[0:8, :], 3, 0)
    down = pltpu.roll(main, 3, 0)
    up = pltpu.roll(main, 35, 0)
    low_case = jnp.concatenate([jnp.where(sub < 3, tile, down[0:8]), down[8:40]], axis=0)
    high_case = jnp.concatenate(
        [up[0:32], jnp.where((sub >= 3) & (sub < 6), tile, up[32:40])], axis=0
    )
    image = jnp.where(lower, low_case, high_case)
    lanes = lax.broadcasted_iota(jnp.int32, (40, 128), 1)
    scale = 1.0 / float(STEPS * 16) ** 0.5
    shifted = pltpu.roll(image, 3, 1)
    image_a = jnp.where(lanes < 3, turned, shifted) * scale
    image_b = jnp.where(lanes < 3, shifted, jnp.where(lanes < 6, turned, 0.0)) * scale
    shifted = pltpu.roll(cotangent_rows[...], 3, 1)
    sides = pltpu.roll(turned, 121, 1)
    cot_a = jnp.where(lanes < 1, 0.0, jnp.where(lanes < 3, sides, shifted))
    cot_b = jnp.where(lanes < 3, shifted, jnp.where(lanes < 5, sides, 0.0))
    velocity_all = velocity_wide[...]

    base[...] = jnp.zeros(base.shape, jnp.float32)
    wide_rows = [
        velocity_all,
        jnp.concatenate([image_a, image_b], axis=1),
        jnp.concatenate([cot_a, cot_b], axis=1),
    ]
    for channel, wide in enumerate(wide_rows):
        pieces = {}
        for r in range(38):
            start = LINE * r
            v, offset = start // 128, start % 128
            row = wide[r : r + 1, :]
            if offset:
                row = pltpu.roll(row, offset, 1)
            pieces.setdefault(v, []).append(row[:, 0:128])
            pieces.setdefault(v + 1, []).append(row[:, 128:256])
        for v, found in pieces.items():
            total = found[0]
            for piece in found[1:]:
                total = total + piece
            base[channel : channel + 1, SIDE + 128 * v : SIDE + 128 * v + 128] = total

    parts = [(p * PART, slice(p * PART, (p + 1) * PART)) for p in range(FLAT // PART)]
    for first, cut in parts:
        at = (lax.broadcasted_iota(jnp.int32, (8, PART), 1) + first).astype(jnp.float32)
        row_of = jnp.floor((at + 0.5) * (1.0 / LINE)).astype(jnp.int32)
        col_of = lax.broadcasted_iota(jnp.int32, (8, PART), 1) + first - LINE * row_of
        grid_row, grid_col = row_of + row_base[0], col_of + col_base[0]
        mask = (row_of < 38) & (col_of < 134)
        mask = mask & (grid_row >= 0) & (grid_row < 1024) & (grid_col >= 0) & (grid_col < 1024)
        inside[:, cut] = jnp.where(mask, 1.0, 0.0)
        mask = (row_of >= 3) & (row_of < 35) & (col_of >= 3) & (col_of < 131)
        own[:, cut] = jnp.where(mask, 1.0, 0.0)
    all_rows = slice(0, 8)
    padding = jnp.zeros((8, PART), jnp.float32)
    for first, cut in parts:
        gathered = [window(base, all_rows, first, PART, shift) for shift in TAPS]
        high, low = split(jnp.concatenate(gathered + [padding], axis=0))
        taps[0:80, cut] = high
        taps[80:160, cut] = low
        result = mul(first_w[...], taps[:, cut])
        result = result[0:64] + result[64:128]
        value = result[0:CH]
        pulled = jax.nn.sigmoid(value)
        slope_one_d[:, cut] = pulled * (1.0 + value * (1.0 - pulled))
        mask = inside[:, cut] > 0.0
        mask = jnp.concatenate([mask] * 4, axis=0)
        hidden = jnp.where(mask, value * pulled, 0.0)
        hidden_one[:, SIDE + first : SIDE + first + PART] = hidden
        before[:, cut] = result[CH : 2 * CH]
        high, low = split(hidden)
        packed[0:32, cut] = high
        packed[32:64, cut] = low
        packed[64:96, cut] = high
    edge = jnp.zeros((CH, SIDE), jnp.float32)
    hidden_one[:, 0:SIDE] = edge
    hidden_one[:, SIDE + FLAT :] = edge
    zero_edge = jnp.zeros((9 * CH, SIDE), jnp.float32)
    products[:, 0:SIDE] = zero_edge
    products[:, SIDE + FLAT :] = zero_edge
    last_products[:, 0:SIDE] = jnp.zeros((16, SIDE), jnp.float32)
    last_products[:, SIDE + FLAT :] = jnp.zeros((16, SIDE), jnp.float32)

    for first, cut in parts:
        products[:, SIDE + first : SIDE + first + PART] = mul(middle_w[...], packed[:, cut])
    for first, cut in parts:
        mask = inside[:, cut] > 0.0
        here = own[:, cut] > 0.0
        for g in range(4):
            total = None
            for tap, shift in enumerate(TAPS):
                piece = window(
                    products, slice(tap * CH + 8 * g, tap * CH + 8 * g + 8), first, PART, shift
                )
                total = piece if total is None else total + piece
            pulled = jax.nn.sigmoid(total)
            rows = slice(8 * g, 8 * g + 8)
            hidden = jnp.where(mask, total * pulled, 0.0)
            slope = jnp.where(
                mask, before[rows, cut] * (pulled * (1.0 + total * (1.0 - pulled))), 0.0
            )
            pairs[rows, cut] = hidden
            slope_own[rows, cut] = slope
        hidden = pairs[:, cut]
        slope = slope_own[:, cut]
        high, low = split(hidden)
        packed_two[0:32, cut] = high
        packed_two[32:64, cut] = low
        packed_two[64:96, cut] = high
        here = jnp.concatenate([here] * 4, axis=0)
        high, low = split(jnp.where(here, hidden, 0.0))
        own_terms[32:64, cut] = high
        own_terms[96:128, cut] = low
        high, low = split(slope)
        packed_slope[0:32, cut] = high
        packed_slope[32:64, cut] = low
        packed_slope[64:96, cut] = high
        last_products[:, SIDE + first : SIDE + first + PART] = mul(last_w[...], packed_two[:, cut])

    wide_sub = lax.broadcasted_iota(jnp.int32, (8, PART), 0)
    for first, cut in parts:
        total = jnp.zeros((8, PART), jnp.float32)
        for tap, shift in enumerate(TAPS):
            rows = slice(0, 8) if tap < 8 else slice(8, 16)
            piece = window(last_products, rows, first, PART, shift)
            total = total + jnp.where(wide_sub == tap % 8, piece, 0.0)
        updates[0:1, cut] = jnp.sum(total, axis=0, keepdims=True)
    velocity_here = pltpu.roll(velocity_all, 253, 1)[:, 0:128]
    for r in range(32):
        start = LINE * (r + 3) + 3
        v, offset = start // 128, start % 128
        row = updates[0:1, 128 * v : 128 * v + 256]
        if offset:
            row = pltpu.roll(row, 256 - offset, 1)
        new_velocity[r : r + 1, :] = velocity_here[r + 3 : r + 4] + row[:, 0:128]

    for first, cut in parts:
        products[:, SIDE + first : SIDE + first + PART] = mul(back_w[...], packed_slope[:, cut])
    for first, cut in parts:
        here = own[:, cut] > 0.0
        for g in range(4):
            total = None
            for tap, shift in enumerate(TAPS):
                piece = window(
                    products, slice(tap * CH + 8 * g, tap * CH + 8 * g + 8), first, PART, -shift
                )
                total = piece if total is None else total + piece
            rows = slice(8 * g, 8 * g + 8)
            pairs[rows, cut] = jnp.where(here, total * slope_one_d[rows, cut], 0.0)
        high, low = split(pairs[:, cut])
        own_terms[0:32, cut] = high
        own_terms[64:96, cut] = low

    middle_sum = jnp.zeros((CH, 9 * CH), jnp.float32)
    outer_sum = jnp.zeros((64, 80), jnp.float32)
    for first, cut in parts:
        here = jnp.concatenate([own[:, cut] > 0.0] * 4, axis=0)
        shifted = jnp.concatenate(
            [window(hidden_one, slice(0, CH), first, PART, shift) for shift in TAPS], axis=0
        )
        high, low = split(shifted)
        slope_high, slope_low = split(jnp.where(here, slope_own[:, cut], 0.0))
        both = mul_t(jnp.concatenate([slope_high, slope_low], axis=0), high)
        middle_sum = middle_sum + (both[0:CH] + both[CH:] + mul_t(slope_high, low))
        terms = own_terms[:, cut]
        both = mul_t(terms, taps[0:80, cut])
        outer_sum = outer_sum + (both[0:64] + both[64:128] + mul_t(terms[0:64], taps[80:160, cut]))
    blank = jnp.zeros((CH, 48), jnp.float32)
    first_sum = jnp.concatenate([outer_sum[0:CH], blank], axis=1)
    last_sum = jnp.concatenate([outer_sum[CH:64], blank], axis=1)
    lanes = lax.broadcasted_iota(jnp.int32, (CH, 128), 1)
    tail = jnp.concatenate([middle_sum[:, 256:288], jnp.zeros((CH, 96), jnp.float32)], axis=1)
    for tap in range(9):
        moved = pltpu.roll(first_sum, (32 + 2 * tap - 8 * tap) % 128, 1)
        tail = jnp.where((lanes >= 32 + 2 * tap) & (lanes < 34 + 2 * tap), moved, tail)
    grads[0:CH, 0:256] = middle_sum[:, 0:256]
    grads[0:CH, 256:384] = tail
    columns = jnp.transpose(jnp.concatenate([last_sum, jnp.zeros((96, 128), jnp.float32)], axis=0))
    line = lax.broadcasted_iota(jnp.int32, (1, 128), 1) // 32
    for part in range(3):
        row = jnp.zeros((1, 128), jnp.float32)
        for q in range(4):
            tap = 4 * part + q
            if tap < 9:
                at = 8 * (8 - tap) + 2
                row = jnp.where(line == q, pltpu.roll(columns[at : at + 1], 32 * q, 1), row)
        grads[CH : CH + 1, 128 * part : 128 * part + 128] = row
    grads[CH + 1 : CH + 8, :] = jnp.zeros((7, 384), jnp.float32)


def last_kernel(one, other, grad_in, grad_mid, grad_out):
    total = one[...] + other[...]
    grad_mid[...] = total[0:CH, 0:288]
    grad_in[...] = jnp.transpose(total[0:CH, 256:384])[32:50]
    grad_out[...] = total[CH : CH + 1, 0:288]


def vmem():
    return pl.BlockSpec(memory_space=pltpu.VMEM)


def anywhere():
    return pl.BlockSpec(memory_space=pl.ANY)


def in_hbm():
    return pl.BlockSpec(memory_space=pltpu.HBM)


def smem():
    return pl.BlockSpec(memory_space=pltpu.SMEM)


def f32(*shape):
    return jax.ShapeDtypeStruct(shape, jnp.float32)


def scratch(*shape, dtype=jnp.float32):
    return pltpu.VMEM(shape, dtype)


def call(kernel, in_specs, out_shape, scratch_shapes, *operands, out_specs=None):
    many = isinstance(out_shape, tuple)
    default = tuple(vmem() for _ in out_shape) if many else vmem()
    return pl.pallas_call(
        kernel,
        in_specs=in_specs,
        out_specs=default if out_specs is None else out_specs,
        out_shape=out_shape,
        scratch_shapes=scratch_shapes,
        compiler_params=pltpu.CompilerParams(vmem_limit_bytes=vmem_limit),
    )(*operands)


def stacked_weights(weights):
    high = weights.astype(jnp.bfloat16)
    low = (weights - lax.reduce_precision(weights, 8, 7)).astype(jnp.bfloat16)
    return high, low


def three_terms(weights):
    high, low = stacked_weights(weights)
    return jnp.concatenate([high, high, low], axis=1)


def over_pairs(x, axis, groups):
    return x + lax.ppermute(x, axis, [(a, b) for a, b in groups] + [(b, a) for a, b in groups])


def over_fours(x, axis, groups):
    near, far, cross = (
        lax.ppermute(x, axis, [(group[i], group[i ^ turn]) for group in groups for i in range(4)])
        for turn in (1, 2, 3)
    )
    return (x + near) + (far + cross)


def on_device(
    velocity,
    wave_now,
    wave_before,
    adjoint_last,
    adjoint_after,
    wavelet,
    source_col,
    rec_first,
    rec_last,
    rec_count,
    observed,
    conv_in,
    conv_mid,
    conv_out,
    cotangent,
):
    core = lax.axis_index(CORE)
    chip = lax.axis_index(CHIPS)
    cell = lax.axis_index(CELL)
    chips = lax.axis_size(CHIPS)
    core_id, chip_id, cell_id = (x.reshape(1).astype(jnp.int32) for x in (core, chip, cell))
    mine_w, given_w, mine_a, given_a = call(
        pack_kernel,
        [smem()] + [vmem()] * 6,
        (f32(WAVES * 8, 128), f32(WAVES * 8, 128), f32(CHIP * 8, 128), f32(CHIP * 8, 128)),
        [],
        core_id,
        wave_now,
        wave_before,
        adjoint_last,
        adjoint_after,
        velocity,
        cotangent,
    )
    swap = [(0, 1), (1, 0)]
    up = [(i, i + 1) for i in range(chips - 1)]
    down = [(i + 1, i) for i in range(chips - 1)]
    theirs_w = lax.ppermute(given_w, CORE, swap)
    theirs_a = lax.ppermute(given_a, CORE, swap)
    waves = jnp.concatenate([mine_w, theirs_w]).reshape(2 * WAVES, 8, 128)
    low = lax.ppermute(waves, CHIPS, up)
    high = lax.ppermute(waves, CHIPS, down)
    waves_kept, mine_a, theirs_a, source_col, rec_first, rec_last, rec_count, observed = (
        lax.optimization_barrier(
            (waves, mine_a, theirs_a, source_col, rec_first, rec_last, rec_count, observed)
        )
    )
    adjoints = jnp.concatenate([mine_a, theirs_a]).reshape(2 * CHIP, 8, 128)
    source, counts, recorded = call(
        receiver_kernel,
        [smem()] * 6 + [vmem()],
        (f32(8, 128), f32(8, 128), f32(STEPS * 8, 128)),
        [],
        core_id,
        chip_id,
        source_col,
        rec_first,
        rec_last,
        rec_count,
        observed,
    )
    adjoints, counts, recorded, source, low, high = lax.optimization_barrier(
        (adjoints, counts, recorded, source, low, high)
    )
    low_adjoint = lax.ppermute(adjoints, CHIPS, up)
    high_adjoint = lax.ppermute(adjoints, CHIPS, down)

    stored, speeds, velocity_rows, cot_rows = call(
        forward_kernel,
        [smem()] * 2 + [vmem(), in_hbm(), anywhere(), in_hbm()],
        (f32(STEPS, CHIP, 8, 128), f32(WIDE, 8, 128), f32(40, 8, 128), f32(40, 128)),
        [
            scratch(2, WIDE, 8, 128),
            scratch(WIDE, 8, 128),
            scratch(10, 8, 128),
            pltpu.SemaphoreType.DMA((18,)),
            pltpu.SemaphoreType.DMA((4,)),
            pltpu.SemaphoreType.DMA((2,)),
        ],
        core_id,
        wavelet,
        source,
        low,
        waves_kept,
        high,
        out_specs=(in_hbm(), vmem(), vmem(), vmem()),
    )
    pieces = call(
        adjoint_kernel,
        [smem()] * 2 + [vmem()] * 2 + [in_hbm(), anywhere(), in_hbm(), vmem(), in_hbm(), vmem()],
        f32(16, 48, 128),
        [
            scratch(2, WIDE, 8, 128),
            scratch(CHIP, 8, 128),
            scratch(8, 128, 128),
            scratch(2, CHIP, 8, 128),
            pltpu.SemaphoreType.DMA((12,)),
            pltpu.SemaphoreType.DMA((2,)),
        ],
        core_id,
        cell_id,
        counts,
        recorded.reshape(STEPS, 8, 128),
        low_adjoint,
        adjoints,
        high_adjoint,
        speeds,
        stored,
        cot_rows,
    )
    pieces, velocity_rows, conv_in, conv_mid, conv_out = lax.optimization_barrier(
        (pieces, velocity_rows, conv_in, conv_mid, conv_out)
    )
    lower = core == 0
    velocity_wide = lax.dynamic_slice_in_dim(
        jnp.pad(velocity_rows.reshape(40, 1024), ((0, 0), (3, 253))), 128 * cell, 256, 1
    )
    velocity_wide = jnp.where(jnp.arange(256)[None, :] < 134, velocity_wide, 0.0)
    first = jnp.pad(conv_in.reshape(CH, 9, 2), ((0, 0), (0, 1), (0, 6))).reshape(CH, 80)
    pulling = jnp.pad(
        conv_out.reshape(9, CH)[::-1].T[:, :, None], ((0, 0), (0, 1), (2, 5))
    ).reshape(CH, 80)
    first_high, first_low = stacked_weights(jnp.concatenate([first, pulling]))
    first_w = jnp.concatenate(
        [
            jnp.concatenate([first_high, first_high], axis=1),
            jnp.concatenate([first_low, jnp.zeros_like(first_low)], axis=1),
        ]
    )
    middle = conv_mid.reshape(CH, 9, CH)
    middle_w = three_terms(middle.transpose(1, 0, 2).reshape(9 * CH, CH))
    back_w = three_terms(middle.transpose(1, 2, 0).reshape(9 * CH, CH))
    last_w = three_terms(jnp.pad(conv_out.reshape(9, CH), ((0, 7), (0, 0))))

    summed = jnp.sum(lax.all_to_all(pieces, SUMMED, 0, 0, tiled=True), axis=0)
    edge_rows = jnp.concatenate([jnp.where(lower, summed[0:8], summed[32:40]), summed[40:48]])
    bands = lax.axis_size(BAND)
    outward = [(b, b - 1) for b in range(2, bands, 2)] + [(b, b + 1) for b in range(1, bands - 1, 2)]
    arrived = lax.ppermute(edge_rows, BAND, outward)

    bf16 = jnp.bfloat16
    new_velocity, grads = call(
        network_kernel,
        [smem()] * 3 + [vmem()] * 8,
        (f32(32, 128), f32(CH + 8, 384)),
        [
            scratch(8, FLAT + 2 * SIDE),
            scratch(160, FLAT, dtype=bf16),
            scratch(96, FLAT, dtype=bf16),
            scratch(CH, FLAT),
            scratch(CH, FLAT),
            scratch(9 * CH, FLAT + 2 * SIDE),
            scratch(16, FLAT + 2 * SIDE),
            scratch(CH, FLAT),
            scratch(CH, FLAT + 2 * SIDE),
            scratch(CH, FLAT),
            scratch(96, FLAT, dtype=bf16),
            scratch(96, FLAT, dtype=bf16),
            scratch(128, FLAT, dtype=bf16),
            scratch(8, FLAT),
            scratch(8, FLAT),
            scratch(8, FLAT),
        ],
        core_id,
        (64 * chip + 32 * core - 3).reshape(1).astype(jnp.int32),
        (128 * cell - 3).reshape(1).astype(jnp.int32),
        summed,
        arrived,
        velocity_wide,
        cot_rows,
        first_w,
        middle_w,
        back_w,
        last_w,
    )
    total = over_pairs(grads, CORE, [(0, 1)])
    total = over_fours(total, "shot", [(0, 1, 2, 3)])
    total = over_fours(total, ("band_0", "net"), [(0, 1, 2, 3)])
    total = over_fours(total, "band_1", [(0, 1, 2, 3), (4, 5, 6, 7)])
    other = lax.ppermute(total, "band_1", [(i, 7 - i) for i in range(8)])
    grad_in, grad_mid, grad_out = call(
        last_kernel,
        [vmem()] * 2,
        (f32(18, CH), f32(CH, 9 * CH), f32(1, 9 * CH)),
        [],
        total,
        other,
    )
    return new_velocity, grad_in.T, grad_mid, grad_out


def solution(mesh):
    split_mesh = Mesh(
        mesh.devices.reshape(mesh.shape["shot"], 2, 8, 2, mesh.shape["net"]),
        ("shot", "band_0", "band_1", "band_2", "net"),
    )
    placed = (
        P(BAND, None),
        P(CELL, BAND, None),
        P(CELL, BAND, None),
        P(CELL, BAND, None),
        P(CELL, BAND, None),
        P(CELL, None),
        P(CELL),
        P(CELL),
        P(CELL),
        P(CELL),
        P(CELL, None, None),
        P(),
        P(),
        P(),
        P(BAND, CELL),
    )
    return jax.shard_map(
        on_device,
        mesh=split_mesh,
        in_specs=placed,
        out_specs=(P(BAND, CELL), P(), P(), P()),
        check_vma=False,
    )
```
